32 devices in a mesh: space: 16 (over z, x, core), tensor: 2 (over y).
Axes of the slice: x: 2, y: 2, z: 4, core: 2. Of those that a mesh axis runs over, the one named last changes fastest.
Arguments:
- tokens: float32 [2, 128, 128, 2048], P(None, 'space', None, 'tensor'), may hold values from -6 to 6
- in_gain: float32 [2048], replicated, may hold values from 0.25 to 1.75
- w_inner: bfloat16 [2048, 3072], P(None, 'tensor'), may hold values from -0.125 to 0.125
- w_bc: bfloat16 [2048, 256], replicated, may hold values from -0.03125 to 0.03125
- w_step: bfloat16 [2048, 48], P(None, 'tensor'), may hold values from -0.125 to 0.125
- step_bias: float32 [48], P('tensor'), may hold values from -3 to 0
- decay_rate: float32 [48], P('tensor'), may hold values from 0.02 to 2
- skip: float32 [48], P('tensor'), may hold values from 0.5 to 2
- norm_gain: float32 [3072], P('tensor'), may hold values from 0.25 to 1.75
- w_out: bfloat16 [3072, 2048], P('tensor'), may hold values from -0.109375 to 0.109375
Outputs:
- mixed: bfloat16 [2, 128, 128, 2048], P(None, 'space', None, 'tensor')
The draws below stay inside these ranges and needn't reach their ends.
All inputs are finite; a program needn't handle non-finite values.
Results may differ from the reference program's by a relative error of at most 0.011.
Values may be sent and summed in bfloat16 or wider, within the bound.
A program may use at most 128 MiB of HBM per device.

```python
import math
import jax
import jax.numpy as jnp
from jax import lax

D = 2048
HEADS = 48
HEAD_DIM = 64
STATE = 128
NORM_HEADS = 6
H = 128
W = 128
IMAGES = 2
INNER = 3072


def shard_levels(own_key, shape, cuts, smallest, high):
    def one(dim, shards_of):
        heights = jax.random.uniform(jax.random.fold_in(jax.random.fold_in(own_key, 6), dim), (shards_of,), jnp.float32, smallest / len(cuts), high / len(cuts))
        return jnp.repeat(jnp.exp(heights), shape[dim] // shards_of).reshape((-1,) + (1,) * (len(shape) - dim - 1))

    loudness = one(*cuts[0])
    for cut in cuts[1:]:
        loudness = loudness * one(*cut)
    return loudness


def noise(stream_key, shape, spread, reach, shards=(), dtype=jnp.bfloat16):
    level = shard_levels(stream_key, shape, shards, -0.22, 0.18) if shards else 1.0
    entries = jax.random.normal(stream_key, shape, jnp.float32) * spread * level
    return jnp.minimum(jnp.maximum(entries, -reach), reach).astype(dtype)


def setup_inputs(seed: int = 0) -> dict:
    arg_keys = jax.random.split(jax.random.key(seed), 11)
    tokens = noise(arg_keys[0], (IMAGES, H, W, D), 1.0, 6.0, ((1, 16), (3, 2)), jnp.float32)
    in_gain = jnp.clip(1.0 + 0.15 * jax.random.normal(arg_keys[1], (D,), jnp.float32), 0.25, 1.75)
    w_inner = noise(arg_keys[2], (D, INNER), D ** -0.5, 0.125, ((1, 2),))
    w_bc = noise(arg_keys[3], (D, 2 * STATE), (D * 16) ** -0.5, 0.03125)
    w_step = noise(arg_keys[4], (D, HEADS), D ** -0.5, 0.125, ((1, 2),))
    step_bias = jnp.clip(-3.0 + 3.0 * jax.random.uniform(arg_keys[5], (HEADS,), jnp.float32) ** shard_levels(arg_keys[5], (HEADS,), ((0, 2),), -0.2, 0.2), -3.0, 0.0)
    decay_rate = jnp.clip(jnp.exp(math.log(2.0) - 4.6051702 * jax.random.uniform(arg_keys[6], (HEADS,), jnp.float32) ** shard_levels(arg_keys[6], (HEADS,), ((0, 2),), -0.2, 0.2)), 0.02, 2.0)
    skip = jnp.clip(0.5 + 1.5 * jax.random.uniform(arg_keys[7], (HEADS,), jnp.float32) ** shard_levels(arg_keys[7], (HEADS,), ((0, 2),), -0.2, 0.2), 0.5, 2.0)
    norm_gain = jnp.clip(1.0 + 0.15 * jax.random.normal(arg_keys[8], (INNER,), jnp.float32), 0.25, 1.75)
    w_out = noise(arg_keys[9], (INNER, D), INNER ** -0.5, 0.109375, ((0, 2),))
    return {"tokens": tokens, "in_gain": in_gain, "w_inner": w_inner, "w_bc": w_bc, "w_step": w_step, "step_bias": step_bias, "decay_rate": decay_rate, "skip": skip, "norm_gain": norm_gain, "w_out": w_out}


EPS = 1e-05

def kernel(logdecay):
    running = jnp.cumsum(logdecay, axis=-1)
    length = logdecay.shape[-1]
    place = jnp.arange(length)
    lower = place[:, None] >= place[None, :]
    upper = place[:, None] <= place[None, :]
    later = running[..., :, None] - running[..., None, :]
    shifted = running - logdecay
    earlier = shifted[..., None, :] - shifted[..., :, None]
    forward = jnp.exp(jnp.where(lower, later, -jnp.inf))
    backward = jnp.exp(jnp.where(upper, earlier, -jnp.inf))
    return forward + backward

def bidirectional(values, maps, logdecay):
    seqs, length, channels = values.shape
    heads = logdecay.shape[-1]
    in_map = maps[:, :, :STATE].astype(jnp.float32)
    out_map = maps[:, :, STATE:].astype(jnp.float32)
    scores = jnp.einsum('sln,smn->slm', out_map, in_map)
    split_values = values.reshape(seqs, length, heads, HEAD_DIM)
    decays = logdecay.astype(jnp.float32)

    def one_head(head):
        weights = (scores * kernel(decays[:, :, head])).astype(jnp.bfloat16)
        return jnp.einsum('slm,smp->slp', weights.astype(jnp.float32), split_values[:, :, head].astype(jnp.float32))
    outs = lax.map(one_head, jnp.arange(heads))
    return jnp.transpose(outs, (1, 2, 0, 3)).reshape(seqs, length, channels)

def reference(tokens, in_gain, w_inner, w_bc, w_step, step_bias, decay_rate, skip, norm_gain, w_out):
    rounded = tokens.astype(jnp.bfloat16).astype(jnp.float32)
    scale = lax.rsqrt(lax.optimization_barrier(jnp.mean(rounded * rounded, axis=-1, keepdims=True)) + EPS)
    normed = (rounded * scale * in_gain).astype(jnp.bfloat16)
    flat = normed.reshape(-1, D)
    inner = jnp.dot(flat, w_inner, preferred_element_type=jnp.float32).astype(jnp.bfloat16)
    maps = jnp.dot(flat, w_bc, preferred_element_type=jnp.float32).astype(jnp.bfloat16)
    step = jax.nn.softplus(jnp.dot(flat, w_step, preferred_element_type=jnp.float32) + step_bias)
    logdecay = (-decay_rate * step).astype(jnp.bfloat16)
    value = (inner.reshape(-1, HEADS, HEAD_DIM).astype(jnp.float32) * step[:, :, None]).reshape(-1, INNER).astype(jnp.bfloat16)
    value = value.reshape(IMAGES, H, W, INNER)
    maps = maps.reshape(IMAGES, H, W, 2 * STATE)
    logdecay = logdecay.reshape(IMAGES, H, W, HEADS)
    row_out = bidirectional(value.reshape(IMAGES * H, W, INNER), maps.reshape(IMAGES * H, W, 2 * STATE), logdecay.reshape(IMAGES * H, W, HEADS)).reshape(IMAGES, H, W, INNER)
    col_value = jnp.transpose(value, (0, 2, 1, 3)).reshape(IMAGES * W, H, INNER)
    col_maps = jnp.transpose(maps, (0, 2, 1, 3)).reshape(IMAGES * W, H, 2 * STATE)
    col_decay = jnp.transpose(logdecay, (0, 2, 1, 3)).reshape(IMAGES * W, H, HEADS)
    column_out = bidirectional(col_value, col_maps, col_decay).reshape(IMAGES, W, H, INNER)
    column_out = jnp.transpose(column_out, (0, 2, 1, 3)).astype(jnp.bfloat16)
    skip_wide = jnp.repeat(skip, HEAD_DIM)
    total = row_out + column_out.astype(jnp.float32) + skip_wide * inner.reshape(IMAGES, H, W, INNER).astype(jnp.float32)
    group = NORM_HEADS * HEAD_DIM
    grouped = total.reshape(IMAGES, H, W, INNER // group, group)
    norm_scale = lax.rsqrt(lax.optimization_barrier(jnp.mean(grouped * grouped, axis=-1, keepdims=True)) + EPS)
    gated = (grouped * norm_scale).reshape(IMAGES, H, W, INNER) * norm_gain
    gated = gated.astype(jnp.bfloat16)
    mixer = jnp.dot(gated.reshape(-1, INNER), w_out, preferred_element_type=jnp.float32).reshape(IMAGES, H, W, D)
    return (tokens + mixer).astype(jnp.bfloat16)
```

```python
import functools

import jax
import jax.numpy as jnp
from jax import lax
from jax.experimental import pallas as pl
from jax.experimental.pallas import tpu as pltpu
from jax.sharding import PartitionSpec as P

HEAD_DIM = 64
STATE = 128
NORM_HEADS = 6


EPS = 1e-05


def kernel(logdecay):
    running = jnp.cumsum(logdecay, axis=-1)
    length = logdecay.shape[-1]
    place = jnp.arange(length)
    lower = place[:, None] >= place[None, :]
    upper = place[:, None] <= place[None, :]
    later = running[..., :, None] - running[..., None, :]
    shifted = running - logdecay
    earlier = shifted[..., None, :] - shifted[..., :, None]
    forward = jnp.exp(jnp.where(lower, later, -jnp.inf))
    backward = jnp.exp(jnp.where(upper, earlier, -jnp.inf))
    return forward + backward


def scan_grid(values, maps, logdecay, along_rows):
    heads = logdecay.shape[-1]
    in_map = maps[..., :STATE]
    out_map = maps[..., STATE:]
    split_values = values.reshape(values.shape[:3] + (heads, HEAD_DIM))
    if along_rows:
        scores = jnp.einsum("ialn,iamn->ialm", out_map, in_map, preferred_element_type=jnp.float32)
        decays = jnp.moveaxis(logdecay.astype(jnp.float32), 3, 2)
    else:
        scores = jnp.einsum("ilan,iman->ialm", out_map, in_map, preferred_element_type=jnp.float32)
        decays = jnp.transpose(logdecay.astype(jnp.float32), (0, 2, 3, 1))
    weights = (scores[:, :, None] * kernel(decays)).astype(jnp.bfloat16)
    if along_rows:
        result = jnp.einsum(
            "iahlm,iamhp->ialhp", weights, split_values, preferred_element_type=jnp.float32
        )
    else:
        result = jnp.einsum(
            "iahlm,imahp->ilahp", weights, split_values, preferred_element_type=jnp.float32
        )
    return result.reshape(values.shape)


def on_device(
    tokens, in_gain, w_inner, w_bc, w_step, step_bias, decay_rate, skip, norm_gain, w_out
):
    whole = lax.all_gather(tokens.astype(jnp.bfloat16), "tensor", axis=3, tiled=True)
    rounded = whole.astype(jnp.float32)
    scale = lax.rsqrt(jnp.mean(rounded * rounded, axis=-1, keepdims=True) + EPS)
    normed = (rounded * scale * in_gain).astype(jnp.bfloat16)
    inner = jnp.einsum("irwd,dc->irwc", normed, w_inner, preferred_element_type=jnp.float32).astype(
        jnp.bfloat16
    )
    maps = jnp.einsum("irwd,dc->irwc", normed, w_bc, preferred_element_type=jnp.float32).astype(
        jnp.bfloat16
    )
    step = jax.nn.softplus(
        jnp.einsum("irwd,dc->irwc", normed, w_step, preferred_element_type=jnp.float32) + step_bias
    )
    logdecay = (-decay_rate * step).astype(jnp.bfloat16)
    heads_local = w_step.shape[1]
    lead = inner.shape[:3]
    value = (
        (inner.reshape(lead + (heads_local, HEAD_DIM)).astype(jnp.float32) * step[..., None])
        .reshape(inner.shape)
        .astype(jnp.bfloat16)
    )
    share = maps.shape[3] // lax.axis_size("tensor")
    maps_sent = lax.dynamic_slice_in_dim(maps, lax.axis_index("tensor") * share, share, 3)
    col_value = lax.all_to_all(value, "space", split_axis=2, concat_axis=1, tiled=True)
    col_maps = lax.all_to_all(maps_sent, "space", split_axis=2, concat_axis=1, tiled=True)
    col_decay = lax.all_to_all(logdecay, "space", split_axis=2, concat_axis=1, tiled=True)
    col_maps = lax.all_gather(col_maps, "tensor", axis=3, tiled=True)
    column_out = scan_grid(col_value, col_maps, col_decay, False).astype(jnp.bfloat16)
    column_back = lax.all_to_all(column_out, "space", split_axis=1, concat_axis=2, tiled=True)
    row_out = scan_grid(value, maps, logdecay, True)
    skip_wide = jnp.repeat(skip, HEAD_DIM)
    total = row_out + column_back.astype(jnp.float32) + skip_wide * inner.astype(jnp.float32)
    group = NORM_HEADS * HEAD_DIM
    grouped = total.reshape(lead + (inner.shape[3] // group, group))
    norm_scale = lax.rsqrt(jnp.mean(grouped * grouped, axis=-1, keepdims=True) + EPS)
    gated = ((grouped * norm_scale).reshape(inner.shape) * norm_gain).astype(jnp.bfloat16)
    partial_out = jnp.einsum("irwc,cd->irwd", gated, w_out, preferred_element_type=jnp.float32)
    mixer = lax.psum_scatter(partial_out, "tensor", scatter_dimension=3, tiled=True)
    return (tokens + mixer).astype(jnp.bfloat16)


LANES = 128
SUBLANES = 8
LOG2E = 1.4426950408889634
HALVES = 2
VMEM_LIMIT = 60 * 1024 * 1024


def params(**extra):
    return pltpu.CompilerParams(vmem_limit_bytes=VMEM_LIMIT, **extra)


def resident(shape, index_map):
    return pl.BlockSpec(shape, index_map, pipeline_mode=pl.Buffered(1))


def turn_kernel(rows, tok_ref, out_ref, held):
    width = tok_ref.shape[2]
    for lane in range(tok_ref.shape[3] // LANES):
        part = slice(lane * LANES, (lane + 1) * LANES)
        for row in range(rows):
            held[lane, pl.ds(row, width, stride=rows), :] = tok_ref[0, row, :, part]
        out_ref[:, part] = held[lane].astype(jnp.bfloat16)


def turn(tokens, image, part, width):
    _, rows, _, feats = tokens.shape
    step = width // 2
    return pl.pallas_call(
        functools.partial(turn_kernel, rows),
        grid=(2,),
        in_specs=[
            pl.BlockSpec((1, rows, step, feats), lambda k: (image, 0, 2 * part + k, 0)),
        ],
        out_specs=pl.BlockSpec((step * rows, feats), lambda k: (k, 0)),
        out_shape=jax.ShapeDtypeStruct((width * rows, feats), jnp.bfloat16),
        scratch_shapes=[pltpu.VMEM((feats // LANES, step * rows, LANES), jnp.float32)],
        compiler_params=params(),
        cost_estimate=pl.CostEstimate(
            flops=0, transcendentals=0, bytes_accessed=6 * width * rows * feats
        ),
        name="turn",
    )(tokens)


def project_kernel(
    depth, heads, t_ref, own_ref, other_ref, g_own, g_other, w_own, w_other, m_own, m_other,
    bias_ref, rate_ref, inner_ref, pack_ref,
):
    own = own_ref[...].astype(jnp.float32)
    other = other_ref[...].astype(jnp.float32)
    squares = jnp.sum(own * own, axis=-1, keepdims=True) + jnp.sum(
        other * other, axis=-1, keepdims=True
    )
    scale = lax.rsqrt(squares / depth + EPS)
    n_own = (own * scale * g_own[0]).astype(jnp.bfloat16)
    n_other = (other * scale * g_other[0]).astype(jnp.bfloat16)

    def project(a, b):
        return jnp.dot(n_own, a, preferred_element_type=jnp.float32) + jnp.dot(
            n_other, b, preferred_element_type=jnp.float32
        )

    small = project(m_own[0], m_other[0])
    wide = inner_ref.shape[1]
    step = jax.nn.softplus(small[:, 2 * STATE :] + bias_ref[...])
    pack_ref[:, wide : wide + 2 * STATE] = small[:, : 2 * STATE].astype(jnp.bfloat16)
    pack_ref[:, wide + 2 * STATE :] = (-rate_ref[...] * step).astype(jnp.bfloat16)
    inner = project(w_own[0], w_other[0]).astype(jnp.bfloat16)
    inner_ref[...] = inner
    rows = inner.shape[0]
    low = lax.broadcasted_iota(jnp.int32, (rows, LANES), 1) < HEAD_DIM
    for pair in range(heads // 2):
        part = slice(pair * LANES, (pair + 1) * LANES)
        spread = jnp.where(
            low, step[:, 2 * pair : 2 * pair + 1], step[:, 2 * pair + 1 : 2 * pair + 2]
        )
        pack_ref[:, part] = (inner[:, part].astype(jnp.float32) * spread).astype(jnp.bfloat16)


def project(own, other, in_gain, w_inner, w_small, bias, rate, place, heads):
    rows, feats = own.shape
    wide = w_inner.shape[1]
    small = w_small.shape[1]
    tile = min(rows, 256)
    gains = in_gain.reshape(2, 1, feats)
    w_inner = w_inner.reshape(2, feats, wide)
    w_small = w_small.reshape(2, feats, small)
    row_spec = pl.BlockSpec((tile, feats), lambda i, t: (i, 0))

    def pair(shape):
        return [
            resident((1,) + shape, lambda i, t: (t[0], 0, 0)),
            resident((1,) + shape, lambda i, t: (1 - t[0], 0, 0)),
        ]

    packed = wide + small
    return pl.pallas_call(
        functools.partial(project_kernel, 2 * feats, heads),
        grid_spec=pltpu.PrefetchScalarGridSpec(
            num_scalar_prefetch=1,
            grid=(rows // tile,),
            in_specs=[row_spec, row_spec]
            + pair((1, feats))
            + pair((feats, wide))
            + pair((feats, small))
            + [resident((1, LANES), lambda i, t: (0, 0))] * 2,
            out_specs=[
                pl.BlockSpec((tile, wide), lambda i, t: (i, 0)),
                pl.BlockSpec((tile, packed), lambda i, t: (i, 0)),
            ],
        ),
        out_shape=[
            jax.ShapeDtypeStruct((rows, wide), jnp.bfloat16),
            jax.ShapeDtypeStruct((rows, packed), jnp.bfloat16),
        ],
        compiler_params=params(),
        cost_estimate=pl.CostEstimate(
            flops=4 * rows * feats * packed, transcendentals=0, bytes_accessed=20 * 2**20
        ),
        name="project",
    )(place, own, other, gains, gains, w_inner, w_inner, w_small, w_small, bias, rate)


def scan_sequence(length, heads, in_map, out_map, decay, value_of, store):
    row = lax.broadcasted_iota(jnp.int32, (length, length), 0)
    col = lax.broadcasted_iota(jnp.int32, (length, length), 1)
    lower = row >= col
    ones = jnp.where(lower, 1.0, 0.0).astype(jnp.bfloat16)
    eye = jnp.where(row == col, 1.0, 0.0).astype(jnp.bfloat16)
    scores = lax.dot_general(
        out_map, in_map, (((1,), (1,)), ((), ())), preferred_element_type=jnp.float32
    )
    scores = jnp.where(row == col, scores + scores, scores)
    running = jnp.dot(ones, decay, preferred_element_type=jnp.float32) * LOG2E
    shifted = running - decay.astype(jnp.float32) * LOG2E
    turned = lax.dot_general(
        decay, ones, (((0,), (1,)), ((), ())), preferred_element_type=jnp.float32
    )
    turned_decay = lax.dot_general(
        decay, eye, (((0,), (1,)), ((), ())), preferred_element_type=jnp.float32
    )
    running_row = turned * LOG2E
    shifted_row = running_row - turned_decay * LOG2E
    low = lax.broadcasted_iota(jnp.int32, (length, LANES), 1) < HEAD_DIM
    for pair in range(heads // 2):
        weights = []
        for head in (2 * pair, 2 * pair + 1):
            later = running[:, head : head + 1] - running_row[head : head + 1, :]
            earlier = shifted_row[head : head + 1, :] - shifted[:, head : head + 1]
            decayed = jnp.exp2(jnp.where(lower, later, earlier))
            weights.append((scores * decayed).astype(jnp.bfloat16))
        value = value_of(pair)
        zero = jnp.zeros_like(value)
        stacked = jnp.concatenate(
            [jnp.where(low, value, zero), jnp.where(low, zero, value)], axis=0
        ).astype(jnp.bfloat16)
        store(
            pair,
            jnp.dot(
                jnp.concatenate(weights, axis=1), stacked, preferred_element_type=jnp.float32
            ),
        )


def column_kernel(heads, pack_ref, out_ref):
    owners, _, rows, packed = pack_ref.shape
    length = owners * rows
    wide = out_ref.shape[3]

    def take(start):
        block = pack_ref[:, 0, :, start : start + LANES].astype(jnp.float32)
        return block.reshape(length, LANES)

    def store(pair, result):
        out_ref[:, 0, :, pair * LANES : (pair + 1) * LANES] = result.reshape(
            owners, rows, LANES
        ).astype(jnp.bfloat16)

    scan_sequence(
        length,
        heads,
        take(wide).astype(jnp.bfloat16),
        take(wide + STATE).astype(jnp.bfloat16),
        take(wide + 2 * STATE).astype(jnp.bfloat16),
        lambda pair: take(pair * LANES),
        store,
    )


def scan_cost(sequences, length, heads):
    return pl.CostEstimate(
        flops=8 * sequences * heads * length * length * LANES,
        transcendentals=sequences * heads * length * length,
        bytes_accessed=sequences * length * heads * HEAD_DIM * 6,
    )


def column_scan(pack, heads):
    owners, columns, rows, packed = pack.shape
    wide = heads * HEAD_DIM
    return pl.pallas_call(
        functools.partial(column_kernel, heads),
        grid=(columns,),
        in_specs=[pl.BlockSpec((owners, 1, rows, packed), lambda c: (0, c, 0, 0))],
        out_specs=pl.BlockSpec((owners, 1, rows, wide), lambda c: (0, c, 0, 0)),
        out_shape=jax.ShapeDtypeStruct((owners, columns, rows, wide), jnp.bfloat16),
        compiler_params=params(),
        cost_estimate=scan_cost(columns, owners * rows, heads),
        name="column_scan",
    )(pack)


def row_kernel(rows, heads, *refs):
    packs, out_ref, held = refs[:-2], refs[-2], refs[-1]
    row = pl.program_id(0)
    wide = heads * HEAD_DIM
    tall = packs[0].shape[0]
    length = tall * len(packs) // rows

    @pl.when(row == 0)
    def _():
        for k, pack in enumerate(packs):
            for lane in range(pack.shape[1] // LANES):
                part = slice(lane * LANES, (lane + 1) * LANES)
                held[lane, k * tall : (k + 1) * tall, :] = pack[:, part].astype(jnp.float32)

    def take(lane):
        return held[lane, pl.ds(row, length, stride=rows), :]

    def store(pair, result):
        out_ref[pair, pl.ds(row, length, stride=rows), :] = result

    first = wide // LANES
    scan_sequence(
        length,
        heads,
        take(first).astype(jnp.bfloat16),
        take(first + 1).astype(jnp.bfloat16),
        take(first + 2).astype(jnp.bfloat16),
        take,
        store,
    )


def row_scan(packs, rows, heads):
    tall, packed = packs[0].shape
    total = tall * len(packs)
    wide = heads * HEAD_DIM
    return pl.pallas_call(
        functools.partial(row_kernel, rows, heads),
        grid=(rows,),
        in_specs=[resident((tall, packed), lambda r: (0, 0))] * len(packs),
        out_specs=resident((wide // LANES, total, LANES), lambda r: (0, 0, 0)),
        out_shape=jax.ShapeDtypeStruct((wide // LANES, total, LANES), jnp.float32),
        scratch_shapes=[pltpu.VMEM((packed // LANES, total, LANES), jnp.float32)],
        compiler_params=params(),
        cost_estimate=scan_cost(rows, total // rows, heads),
        name="row_scan",
    )(*packs)


def output_kernel(t_ref, row_ref, col_ref, inner_ref, skip_ref, gain_ref, w_own, w_other, own_ref, send_ref):
    wide = inner_ref.shape[1]
    group = NORM_HEADS * HEAD_DIM
    gated = []
    for start in range(0, wide, group):
        parts = []
        squares = 0.0
        for lane in range(start, start + group, LANES):
            part = slice(lane, lane + LANES)
            total = (
                row_ref[lane // LANES]
                + col_ref[:, part].astype(jnp.float32)
                + skip_ref[:, part] * inner_ref[:, part].astype(jnp.float32)
            )
            parts.append(total)
            squares = squares + total * total
        scale = lax.rsqrt(jnp.sum(squares, axis=-1, keepdims=True) / group + EPS)
        for k, total in enumerate(parts):
            lane = start + k * LANES
            gated.append((total * scale * gain_ref[:, lane : lane + LANES]).astype(jnp.bfloat16))
    gated = jnp.concatenate(gated, axis=1)
    send_ref[...] = jnp.dot(gated, w_other[...], preferred_element_type=jnp.float32).astype(
        jnp.bfloat16
    )
    own_ref[...] = jnp.dot(gated, w_own[...], preferred_element_type=jnp.float32)


def output(row_out, part, col, inner, skip, gain, w_out, place):
    rows, wide = inner.shape
    feats = w_out.shape[1] // 2
    tile = min(rows, 256)
    steps = rows // tile
    row_spec = pl.BlockSpec((tile, wide), lambda i, t: (i, 0))
    out_spec = pl.BlockSpec((tile, feats), lambda i, t: (i, 0))
    return pl.pallas_call(
        output_kernel,
        grid_spec=pltpu.PrefetchScalarGridSpec(
            num_scalar_prefetch=1,
            grid=(steps,),
            in_specs=[
                pl.BlockSpec((wide // LANES, tile, LANES), lambda i, t: (0, part * steps + i, 0)),
                row_spec,
                row_spec,
                resident((1, wide), lambda i, t: (0, 0)),
                resident((1, wide), lambda i, t: (0, 0)),
                resident((wide, feats), lambda i, t: (0, t[0])),
                resident((wide, feats), lambda i, t: (0, 1 - t[0])),
            ],
            out_specs=[out_spec, out_spec],
        ),
        out_shape=[
            jax.ShapeDtypeStruct((rows, feats), jnp.float32),
            jax.ShapeDtypeStruct((rows, feats), jnp.bfloat16),
        ],
        compiler_params=params(),
        cost_estimate=pl.CostEstimate(
            flops=4 * rows * feats * wide, transcendentals=0, bytes_accessed=16 * 2**20
        ),
        name="output",
    )(place, row_out, col, inner, skip, gain, w_out, w_out)


def finish_kernel(rows, own_ref, got_ref, tok_ref, *rest):
    out_ref, held = rest[-2:]
    width = tok_ref.shape[2]
    for lane in range(tok_ref.shape[3] // LANES):
        part = slice(lane * LANES, (lane + 1) * LANES)
        held[lane] = own_ref[:, part] + got_ref[:, part].astype(jnp.float32)
        for row in range(rows):
            out_ref[0, row, :, part] = (
                tok_ref[0, row, :, part] + held[lane, pl.ds(row, width, stride=rows), :]
            ).astype(jnp.bfloat16)


def finish(own, got, tokens, image, part, width, earlier):
    _, rows, _, feats = tokens.shape
    step = width // 2
    flat = pl.BlockSpec((step * rows, feats), lambda k: (k, 0))
    grid_block = pl.BlockSpec((1, rows, step, feats), lambda k: (image, 0, 2 * part + k, 0))
    chained = [] if earlier is None else [earlier]
    return pl.pallas_call(
        functools.partial(finish_kernel, rows),
        grid=(2,),
        in_specs=[flat, flat, grid_block] + [pl.BlockSpec(memory_space=pl.ANY)] * len(chained),
        out_specs=grid_block,
        out_shape=jax.ShapeDtypeStruct(tokens.shape, jnp.bfloat16),
        scratch_shapes=[pltpu.VMEM((feats // LANES, step * rows, LANES), jnp.float32)],
        input_output_aliases={3: 0} if chained else {},
        compiler_params=params(),
        cost_estimate=pl.CostEstimate(
            flops=0, transcendentals=0, bytes_accessed=12 * width * rows * feats
        ),
        name="finish",
    )(own, got, tokens, *chained)


def pipelined(
    owners, tokens, in_gain, w_inner, w_bc, w_step, step_bias, decay_rate, skip, norm_gain, w_out
):
    images, rows, columns, feats = tokens.shape
    heads = w_step.shape[1]
    wide = w_inner.shape[1]
    width = columns // HALVES
    swap = [(0, 1), (1, 0)]
    place = lax.axis_index("tensor").astype(jnp.int32).reshape(1)
    pad = LANES - heads
    w_small = jnp.concatenate([w_bc, jnp.pad(w_step, ((0, 0), (0, pad)))], axis=1)
    bias = jnp.pad(step_bias, (0, pad)).reshape(1, LANES)
    rate = jnp.pad(decay_rate, (0, pad)).reshape(1, LANES)
    skip_wide = jnp.repeat(skip, HEAD_DIM).reshape(1, wide)
    gain = norm_gain.reshape(1, wide)
    chunks = [(image, part) for image in range(images) for part in range(HALVES)]
    own = [turn(tokens, image, part, width) for image, part in chunks]
    other = [lax.ppermute(block, "tensor", swap) for block in own]
    inner, packs, arrived = [], [], []
    for k in range(len(chunks)):
        a, b = project(own[k], other[k], in_gain, w_inner, w_small, bias, rate, place, heads)
        inner.append(a)
        packs.append(b)
        sent = b.reshape(owners, width // owners, rows, b.shape[1])
        arrived.append(lax.all_to_all(sent, "space", split_axis=0, concat_axis=0, tiled=True))
    row_out = [
        row_scan(packs[image * HALVES : (image + 1) * HALVES], rows, heads)
        for image in range(images)
    ]
    result = None
    for k, (image, part) in enumerate(chunks):
        back = lax.all_to_all(
            column_scan(arrived[k], heads), "space", split_axis=0, concat_axis=0, tiled=True
        ).reshape(width * rows, wide)
        kept, send = output(row_out[image], part, back, inner[k], skip_wide, gain, w_out, place)
        got = lax.ppermute(send, "tensor", swap)
        result = finish(kept, got, tokens, image, part, width, result)
    return result


def dispatch(owners, tensor, tokens, *rest):
    heads = rest[3].shape[1]
    rows, columns = tokens.shape[1:3]
    fits = (
        tensor == 2
        and rows == SUBLANES
        and columns % (HALVES * owners) == 0
        and owners * rows == columns == LANES
        and heads % NORM_HEADS == 0
        and heads % 2 == 0
        and heads <= LANES
        and STATE == LANES == 2 * HEAD_DIM
    )
    if fits:
        return pipelined(owners, tokens, *rest)
    return on_device(tokens, *rest)


def solution(mesh):
    body = functools.partial(dispatch, mesh.shape["space"], mesh.shape["tensor"])
    return jax.shard_map(
        body,
        mesh=mesh,
        in_specs=(
            P(None, "space", None, "tensor"),
            P(),
            P(None, "tensor"),
            P(),
            P(None, "tensor"),
            P("tensor"),
            P("tensor"),
            P("tensor"),
            P("tensor"),
            P("tensor", None),
        ),
        out_specs=P(None, "space", None, "tensor"),
        check_vma=False,
    )
```

```python
import functools

import jax
import jax.numpy as jnp
from jax import lax
from jax.experimental import pallas as pl
from jax.experimental.pallas import tpu as pltpu
from jax.sharding import PartitionSpec as P

HEAD_DIM = 64
STATE = 128
NORM_HEADS = 6


EPS = 1e-05


def kernel(logdecay):
    running = jnp.cumsum(logdecay, axis=-1)
    length = logdecay.shape[-1]
    place = jnp.arange(length)
    lower = place[:, None] >= place[None, :]
    upper = place[:, None] <= place[None, :]
    later = running[..., :, None] - running[..., None, :]
    shifted = running - logdecay
    earlier = shifted[..., None, :] - shifted[..., :, None]
    forward = jnp.exp(jnp.where(lower, later, -jnp.inf))
    backward = jnp.exp(jnp.where(upper, earlier, -jnp.inf))
    return forward + backward


def scan_grid(values, maps, logdecay, along_rows):
    heads = logdecay.shape[-1]
    in_map = maps[..., :STATE]
    out_map = maps[..., STATE:]
    split_values = values.reshape(values.shape[:3] + (heads, HEAD_DIM))
    if along_rows:
        scores = jnp.einsum("ialn,iamn->ialm", out_map, in_map, preferred_element_type=jnp.float32)
        decays = jnp.moveaxis(logdecay.astype(jnp.float32), 3, 2)
    else:
        scores = jnp.einsum("ilan,iman->ialm", out_map, in_map, preferred_element_type=jnp.float32)
        decays = jnp.transpose(logdecay.astype(jnp.float32), (0, 2, 3, 1))
    weights = (scores[:, :, None] * kernel(decays)).astype(jnp.bfloat16)
    if along_rows:
        result = jnp.einsum(
            "iahlm,iamhp->ialhp", weights, split_values, preferred_element_type=jnp.float32
        )
    else:
        result = jnp.einsum(
            "iahlm,imahp->ilahp", weights, split_values, preferred_element_type=jnp.float32
        )
    return result.reshape(values.shape)


def on_device(
    tokens, in_gain, w_inner, w_bc, w_step, step_bias, decay_rate, skip, norm_gain, w_out
):
    whole = lax.all_gather(tokens.astype(jnp.bfloat16), "tensor", axis=3, tiled=True)
    rounded = whole.astype(jnp.float32)
    scale = lax.rsqrt(jnp.mean(rounded * rounded, axis=-1, keepdims=True) + EPS)
    normed = (rounded * scale * in_gain).astype(jnp.bfloat16)
    inner = jnp.einsum("irwd,dc->irwc", normed, w_inner, preferred_element_type=jnp.float32).astype(
        jnp.bfloat16
    )
    maps = jnp.einsum("irwd,dc->irwc", normed, w_bc, preferred_element_type=jnp.float32).astype(
        jnp.bfloat16
    )
    step = jax.nn.softplus(
        jnp.einsum("irwd,dc->irwc", normed, w_step, preferred_element_type=jnp.float32) + step_bias
    )
    logdecay = (-decay_rate * step).astype(jnp.bfloat16)
    heads_local = w_step.shape[1]
    lead = inner.shape[:3]
    value = (
        (inner.reshape(lead + (heads_local, HEAD_DIM)).astype(jnp.float32) * step[..., None])
        .reshape(inner.shape)
        .astype(jnp.bfloat16)
    )
    share = maps.shape[3] // lax.axis_size("tensor")
    maps_sent = lax.dynamic_slice_in_dim(maps, lax.axis_index("tensor") * share, share, 3)
    col_value = lax.all_to_all(value, "space", split_axis=2, concat_axis=1, tiled=True)
    col_maps = lax.all_to_all(maps_sent, "space", split_axis=2, concat_axis=1, tiled=True)
    col_decay = lax.all_to_all(logdecay, "space", split_axis=2, concat_axis=1, tiled=True)
    col_maps = lax.all_gather(col_maps, "tensor", axis=3, tiled=True)
    column_out = scan_grid(col_value, col_maps, col_decay, False).astype(jnp.bfloat16)
    column_back = lax.all_to_all(column_out, "space", split_axis=1, concat_axis=2, tiled=True)
    row_out = scan_grid(value, maps, logdecay, True)
    skip_wide = jnp.repeat(skip, HEAD_DIM)
    total = row_out + column_back.astype(jnp.float32) + skip_wide * inner.astype(jnp.float32)
    group = NORM_HEADS * HEAD_DIM
    grouped = total.reshape(lead + (inner.shape[3] // group, group))
    norm_scale = lax.rsqrt(jnp.mean(grouped * grouped, axis=-1, keepdims=True) + EPS)
    gated = ((grouped * norm_scale).reshape(inner.shape) * norm_gain).astype(jnp.bfloat16)
    partial_out = jnp.einsum("irwc,cd->irwd", gated, w_out, preferred_element_type=jnp.float32)
    mixer = lax.psum_scatter(partial_out, "tensor", scatter_dimension=3, tiled=True)
    return (tokens + mixer).astype(jnp.bfloat16)


LANES = 128
SUBLANES = 8
LOG2E = 1.4426950408889634
HALVES = 2
VMEM_LIMIT = 60 * 1024 * 1024


def params(**extra):
    return pltpu.CompilerParams(vmem_limit_bytes=VMEM_LIMIT, **extra)


def resident(shape, index_map):
    return pl.BlockSpec(shape, index_map, pipeline_mode=pl.Buffered(1))


def turn_kernel(rows, tok_ref, out_ref, held):
    width = tok_ref.shape[2]
    for lane in range(tok_ref.shape[3] // LANES):
        part = slice(lane * LANES, (lane + 1) * LANES)
        for row in range(rows):
            held[lane, pl.ds(row, width, stride=rows), :] = tok_ref[0, row, :, part]
        out_ref[:, part] = held[lane].astype(jnp.bfloat16)


def turn(tokens, start, count):
    _, rows, columns, feats = tokens.shape
    step = columns // HALVES // 2
    return pl.pallas_call(
        functools.partial(turn_kernel, rows),
        grid=(2 * count,),
        in_specs=[grid_block(tokens, start)],
        out_specs=pl.BlockSpec((step * rows, feats), lambda k: (k, 0)),
        out_shape=jax.ShapeDtypeStruct((2 * count * step * rows, feats), jnp.bfloat16),
        scratch_shapes=[pltpu.VMEM((feats // LANES, step * rows, LANES), jnp.float32)],
        compiler_params=params(),
        cost_estimate=pl.CostEstimate(
            flops=0, transcendentals=0, bytes_accessed=12 * count * step * rows * feats
        ),
        name="turn",
    )(tokens)


def grid_block(tokens, start):
    _, rows, columns, feats = tokens.shape
    per_image = 2 * HALVES

    def place(k):
        at = 2 * start + k
        return at // per_image, 0, at % per_image, 0

    return pl.BlockSpec((1, rows, columns // per_image, feats), place)


def project_kernel(
    depth, heads, t_ref, own_ref, other_ref, g_own, g_other, w_own, w_other, m_own, m_other,
    bias_ref, rate_ref, inner_ref, pack_ref,
):
    own = own_ref[...].astype(jnp.float32)
    other = other_ref[...].astype(jnp.float32)
    squares = jnp.sum(own * own, axis=-1, keepdims=True) + jnp.sum(
        other * other, axis=-1, keepdims=True
    )
    scale = lax.rsqrt(squares / depth + EPS)
    n_own = (own * scale * g_own[0]).astype(jnp.bfloat16)
    n_other = (other * scale * g_other[0]).astype(jnp.bfloat16)

    def project(a, b):
        return jnp.dot(n_own, a, preferred_element_type=jnp.float32) + jnp.dot(
            n_other, b, preferred_element_type=jnp.float32
        )

    small = project(m_own[0], m_other[0])
    wide = inner_ref.shape[1]
    step = jax.nn.softplus(small[:, 2 * STATE :] + bias_ref[...])
    blocks = pack_ref.shape[:2]

    def put(start, block):
        lanes = block.shape[1]
        pack_ref[:, :, start : start + lanes] = block.astype(jnp.bfloat16).reshape(blocks + (lanes,))

    put(wide, small[:, : 2 * STATE])
    put(wide + 2 * STATE, -rate_ref[...] * step)
    inner = project(w_own[0], w_other[0]).astype(jnp.bfloat16)
    inner_ref[...] = inner
    rows = inner.shape[0]
    low = lax.broadcasted_iota(jnp.int32, (rows, LANES), 1) < HEAD_DIM
    for pair in range(heads // 2):
        part = slice(pair * LANES, (pair + 1) * LANES)
        spread = jnp.where(
            low, step[:, 2 * pair : 2 * pair + 1], step[:, 2 * pair + 1 : 2 * pair + 2]
        )
        put(pair * LANES, inner[:, part].astype(jnp.float32) * spread)


def project(own, other, in_gain, w_inner, w_small, bias, rate, place, heads, owners, count):
    rows, feats = own.shape
    wide = w_inner.shape[1]
    small = w_small.shape[1]
    tile = rows // (2 * count)
    depth = 2 * tile // owners
    gains = in_gain.reshape(2, 1, feats)
    w_inner = w_inner.reshape(2, feats, wide)
    w_small = w_small.reshape(2, feats, small)
    row_spec = pl.BlockSpec((tile, feats), lambda i, t: (i, 0))

    def pair(shape):
        return [
            resident((1,) + shape, lambda i, t: (t[0], 0, 0)),
            resident((1,) + shape, lambda i, t: (1 - t[0], 0, 0)),
        ]

    packed = wide + small
    return pl.pallas_call(
        functools.partial(project_kernel, 2 * feats, heads),
        grid_spec=pltpu.PrefetchScalarGridSpec(
            num_scalar_prefetch=1,
            grid=(rows // tile,),
            in_specs=[row_spec, row_spec]
            + pair((1, feats))
            + pair((feats, wide))
            + pair((feats, small))
            + [resident((1, LANES), lambda i, t: (0, 0))] * 2,
            out_specs=[
                pl.BlockSpec((tile, wide), lambda i, t: (i, 0)),
                pl.BlockSpec((owners // 2, depth, packed), lambda i, t: (i % 2, i // 2, 0)),
            ],
        ),
        out_shape=[
            jax.ShapeDtypeStruct((rows, wide), jnp.bfloat16),
            jax.ShapeDtypeStruct((owners, count * depth, packed), jnp.bfloat16),
        ],
        compiler_params=params(),
        cost_estimate=pl.CostEstimate(
            flops=4 * rows * feats * packed, transcendentals=0, bytes_accessed=20 * 2**20
        ),
        name="project",
    )(place, own, other, gains, gains, w_inner, w_inner, w_small, w_small, bias, rate)


def scan_sequence(length, heads, in_map, out_map, decay, value_of, store):
    row = lax.broadcasted_iota(jnp.int32, (length, length), 0)
    col = lax.broadcasted_iota(jnp.int32, (length, length), 1)
    lower = row >= col
    ones = jnp.where(lower, 1.0, 0.0).astype(jnp.bfloat16)
    eye = jnp.where(row == col, 1.0, 0.0).astype(jnp.bfloat16)
    scores = lax.dot_general(
        out_map, in_map, (((1,), (1,)), ((), ())), preferred_element_type=jnp.float32
    )
    scores = jnp.where(row == col, scores + scores, scores)
    running = jnp.dot(ones, decay, preferred_element_type=jnp.float32) * LOG2E
    shifted = running - decay.astype(jnp.float32) * LOG2E
    turned = lax.dot_general(
        decay, ones, (((0,), (1,)), ((), ())), preferred_element_type=jnp.float32
    )
    turned_decay = lax.dot_general(
        decay, eye, (((0,), (1,)), ((), ())), preferred_element_type=jnp.float32
    )
    running_row = turned * LOG2E
    shifted_row = running_row - turned_decay * LOG2E
    low = lax.broadcasted_iota(jnp.int32, (length, LANES), 1) < HEAD_DIM
    for pair in range(heads // 2):
        weights = []
        for head in (2 * pair, 2 * pair + 1):
            later = running[:, head : head + 1] - running_row[head : head + 1, :]
            earlier = shifted_row[head : head + 1, :] - shifted[:, head : head + 1]
            decayed = jnp.exp2(jnp.where(lower, later, earlier))
            weights.append((scores * decayed).astype(jnp.bfloat16))
        value = value_of(pair)
        zero = jnp.zeros_like(value)
        stacked = jnp.concatenate(
            [jnp.where(low, value, zero), jnp.where(low, zero, value)], axis=0
        ).astype(jnp.bfloat16)
        store(
            pair,
            jnp.dot(
                jnp.concatenate(weights, axis=1), stacked, preferred_element_type=jnp.float32
            ),
        )


def column_kernel(heads, pack_ref, out_ref):
    owners, _, rows, _ = pack_ref.shape
    length = owners * rows
    wide = out_ref.shape[3]

    def take(start):
        block = pack_ref[:, 0, :, start : start + LANES].astype(jnp.float32)
        return block.reshape(length, LANES)

    def store(pair, result):
        out_ref[:, 0, :, pair * LANES : (pair + 1) * LANES] = result.reshape(
            owners, rows, LANES
        ).astype(jnp.bfloat16)

    scan_sequence(
        length,
        heads,
        take(wide).astype(jnp.bfloat16),
        take(wide + STATE).astype(jnp.bfloat16),
        take(wide + 2 * STATE).astype(jnp.bfloat16),
        lambda pair: take(pair * LANES),
        store,
    )


def scan_cost(sequences, length, heads):
    return pl.CostEstimate(
        flops=8 * sequences * heads * length * length * LANES,
        transcendentals=sequences * heads * length * length,
        bytes_accessed=sequences * length * heads * HEAD_DIM * 6,
    )


def column_scan(pack, heads):
    owners, columns, rows, packed = pack.shape
    wide = heads * HEAD_DIM
    return pl.pallas_call(
        functools.partial(column_kernel, heads),
        grid=(columns,),
        in_specs=[pl.BlockSpec((owners, 1, rows, packed), lambda c: (0, c, 0, 0))],
        out_specs=pl.BlockSpec((owners, 1, rows, wide), lambda c: (0, c, 0, 0)),
        out_shape=jax.ShapeDtypeStruct((owners, columns, rows, wide), jnp.bfloat16),
        compiler_params=params(),
        cost_estimate=scan_cost(columns, owners * rows, heads),
        name="column_scan",
    )(pack)


def row_kernel(rows, heads, counts, *refs):
    packs, out_ref, held = refs[:-2], refs[-2], refs[-1]
    image, row = pl.program_id(0), pl.program_id(1)
    wide = heads * HEAD_DIM
    tall = held.shape[1] // HALVES
    length = held.shape[1] // rows
    units = [(pack, k) for pack, count in zip(packs, counts) for k in range(count)]

    for u, (pack, k) in enumerate(units):

        @pl.when((row == 0) & (image == u // HALVES))
        def _(pack=pack, k=k, half=u % HALVES):
            depth = tall // pack.shape[0]
            for lane in range(pack.shape[2] // LANES):
                block = pack[:, k * depth : (k + 1) * depth, lane * LANES : (lane + 1) * LANES]
                held[lane, half * tall : (half + 1) * tall, :] = block.reshape(
                    tall, LANES
                ).astype(jnp.float32)

    def take(lane):
        return held[lane, pl.ds(row, length, stride=rows), :]

    def store(pair, result):
        out_ref[pair, pl.ds(row, length, stride=rows), :] = result

    first = wide // LANES
    scan_sequence(
        length,
        heads,
        take(first).astype(jnp.bfloat16),
        take(first + 1).astype(jnp.bfloat16),
        take(first + 2).astype(jnp.bfloat16),
        take,
        store,
    )


def row_scan(packs, counts, images, rows, columns, heads):
    packed = packs[0].shape[2]
    total = rows * columns
    wide = heads * HEAD_DIM
    return pl.pallas_call(
        functools.partial(row_kernel, rows, heads, counts),
        grid=(images, rows),
        in_specs=[resident(pack.shape, lambda i, r: (0, 0, 0)) for pack in packs],
        out_specs=pl.BlockSpec((wide // LANES, total, LANES), lambda i, r: (0, i, 0)),
        out_shape=jax.ShapeDtypeStruct((wide // LANES, images * total, LANES), jnp.float32),
        scratch_shapes=[pltpu.VMEM((packed // LANES, total, LANES), jnp.float32)],
        compiler_params=params(),
        cost_estimate=scan_cost(images * rows, columns, heads),
        name="row_scan",
    )(*packs)


def output_kernel(t_ref, row_ref, col_ref, inner_ref, skip_ref, gain_ref, w_own, w_other, own_ref, send_ref):
    tall, wide = inner_ref.shape
    group = NORM_HEADS * HEAD_DIM
    gated = []
    for start in range(0, wide, group):
        parts = []
        squares = 0.0
        for lane in range(start, start + group, LANES):
            part = slice(lane, lane + LANES)
            total = (
                row_ref[lane // LANES]
                + col_ref[:, :, part].astype(jnp.float32).reshape(tall, LANES)
                + skip_ref[:, part] * inner_ref[:, part].astype(jnp.float32)
            )
            parts.append(total)
            squares = squares + total * total
        scale = lax.rsqrt(jnp.sum(squares, axis=-1, keepdims=True) / group + EPS)
        for k, total in enumerate(parts):
            lane = start + k * LANES
            gated.append((total * scale * gain_ref[:, lane : lane + LANES]).astype(jnp.bfloat16))
    gated = jnp.concatenate(gated, axis=1)
    send_ref[...] = jnp.dot(gated, w_other[...], preferred_element_type=jnp.float32).astype(
        jnp.bfloat16
    )
    own_ref[...] = jnp.dot(gated, w_own[...], preferred_element_type=jnp.float32)


def output(row_out, start, count, col, inner, skip, gain, w_out, place):
    rows, wide = inner.shape
    feats = w_out.shape[1] // 2
    depth = col.shape[1] // count
    owners = col.shape[0]
    tile = owners * depth // 2
    steps = rows // tile
    row_spec = pl.BlockSpec((tile, wide), lambda i, t: (i, 0))
    out_spec = pl.BlockSpec((tile, feats), lambda i, t: (i, 0))
    return pl.pallas_call(
        output_kernel,
        grid_spec=pltpu.PrefetchScalarGridSpec(
            num_scalar_prefetch=1,
            grid=(steps,),
            in_specs=[
                pl.BlockSpec((wide // LANES, tile, LANES), lambda i, t: (0, 2 * start + i, 0)),
                pl.BlockSpec((owners // 2, depth, wide), lambda i, t: (i % 2, i // 2, 0)),
                row_spec,
                resident((1, wide), lambda i, t: (0, 0)),
                resident((1, wide), lambda i, t: (0, 0)),
                resident((wide, feats), lambda i, t: (0, t[0])),
                resident((wide, feats), lambda i, t: (0, 1 - t[0])),
            ],
            out_specs=[out_spec, out_spec],
        ),
        out_shape=[
            jax.ShapeDtypeStruct((rows, feats), jnp.float32),
            jax.ShapeDtypeStruct((rows, feats), jnp.bfloat16),
        ],
        compiler_params=params(),
        cost_estimate=pl.CostEstimate(
            flops=4 * rows * feats * wide, transcendentals=0, bytes_accessed=16 * 2**20
        ),
        name="output",
    )(place, row_out, col, inner, skip, gain, w_out, w_out)


def finish_kernel(rows, own_ref, got_ref, tok_ref, *rest):
    out_ref, held = rest[-2:]
    width = tok_ref.shape[2]
    for lane in range(tok_ref.shape[3] // LANES):
        part = slice(lane * LANES, (lane + 1) * LANES)
        held[lane] = own_ref[:, part] + got_ref[:, part].astype(jnp.float32)
        for row in range(rows):
            out_ref[0, row, :, part] = (
                tok_ref[0, row, :, part] + held[lane, pl.ds(row, width, stride=rows), :]
            ).astype(jnp.bfloat16)


def finish(own, got, tokens, start, count, earlier):
    _, rows, columns, feats = tokens.shape
    step = columns // HALVES // 2
    flat = pl.BlockSpec((step * rows, feats), lambda k: (k, 0))
    chained = [] if earlier is None else [earlier]
    return pl.pallas_call(
        functools.partial(finish_kernel, rows),
        grid=(2 * count,),
        in_specs=[flat, flat, grid_block(tokens, start)]
        + [pl.BlockSpec(memory_space=pl.ANY)] * len(chained),
        out_specs=grid_block(tokens, start),
        out_shape=jax.ShapeDtypeStruct(tokens.shape, jnp.bfloat16),
        scratch_shapes=[pltpu.VMEM((feats // LANES, step * rows, LANES), jnp.float32)],
        input_output_aliases={3: 0} if chained else {},
        compiler_params=params(),
        cost_estimate=pl.CostEstimate(
            flops=0, transcendentals=0, bytes_accessed=24 * count * step * rows * feats
        ),
        name="finish",
    )(own, got, tokens, *chained)


def pipelined(
    owners, tokens, in_gain, w_inner, w_bc, w_step, step_bias, decay_rate, skip, norm_gain, w_out
):
    images, rows, columns, _ = tokens.shape
    heads = w_step.shape[1]
    wide = w_inner.shape[1]
    swap = [(0, 1), (1, 0)]
    place = lax.axis_index("tensor").astype(jnp.int32).reshape(1)
    pad = LANES - heads
    w_small = jnp.concatenate([w_bc, jnp.pad(w_step, ((0, 0), (0, pad)))], axis=1)
    bias = jnp.pad(step_bias, (0, pad)).reshape(1, LANES)
    rate = jnp.pad(decay_rate, (0, pad)).reshape(1, LANES)
    skip_wide = jnp.repeat(skip, HEAD_DIM).reshape(1, wide)
    gain = norm_gain.reshape(1, wide)
    counts = (1, images * HALVES - 2, 1)
    starts = (0, 1, images * HALVES - 1)
    groups = range(len(counts))
    own, other, inner, packs, arrived, columns_out = [], [], [], [], [], []
    for g in groups:
        own.append(turn(tokens, starts[g], counts[g]))
    for g in groups:
        other.append(lax.ppermute(own[g], "tensor", swap))
    for g in groups:
        a, b = project(
            own[g], other[g], in_gain, w_inner, w_small, bias, rate, place, heads, owners, counts[g]
        )
        inner.append(a)
        packs.append(b)
        arrived.append(lax.all_to_all(b, "space", split_axis=0, concat_axis=0, tiled=True))
    for g in groups:
        block = arrived[g]
        shape = (owners, block.shape[1] // rows, rows, block.shape[2])
        columns_out.append(
            column_scan(block.reshape(shape), heads).reshape(owners, block.shape[1], wide)
        )
    row_out = row_scan(packs, counts, images, rows, columns, heads)
    result = None
    for g in ORDER:
        back = lax.all_to_all(columns_out[g], "space", split_axis=0, concat_axis=0, tiled=True)
        kept, send = output(
            row_out, starts[g], counts[g], back, inner[g], skip_wide, gain, w_out, place
        )
        got = lax.ppermute(send, "tensor", swap)
        result = finish(kept, got, tokens, starts[g], counts[g], result)
    return result


ORDER = (1, 0, 2)


def fits(owners, tensor, tokens, heads):
    images, rows, columns, _ = tokens
    return (
        tensor == 2
        and images * HALVES > 2
        and rows == SUBLANES
        and columns % (HALVES * owners) == 0
        and owners * rows == columns == LANES
        and heads % NORM_HEADS == 0
        and heads % 2 == 0
        and heads <= LANES
        and STATE == LANES == 2 * HEAD_DIM
    )


def dispatch(owners, tensor, tokens, *rest):
    if fits(owners, tensor, tokens.shape, rest[3].shape[1]):
        return pipelined(owners, tokens, *rest)
    return on_device(tokens, *rest)


def solution(mesh):
    body = functools.partial(dispatch, mesh.shape["space"], mesh.shape["tensor"])
    return jax.shard_map(
        body,
        mesh=mesh,
        in_specs=(
            P(None, "space", None, "tensor"),
            P(),
            P(None, "tensor"),
            P(),
            P(None, "tensor"),
            P("tensor"),
            P("tensor"),
            P("tensor"),
            P("tensor"),
            P("tensor", None),
        ),
        out_specs=P(None, "space", None, "tensor"),
        check_vma=False,
    )
```

```python
import functools

import jax
import jax.numpy as jnp
from jax import lax
from jax.experimental import pallas as pl
from jax.experimental.pallas import tpu as pltpu
from jax.sharding import PartitionSpec as P

HEAD_DIM = 64
STATE = 128
NORM_HEADS = 6


EPS = 1e-05


def kernel(logdecay):
    running = jnp.cumsum(logdecay, axis=-1)
    length = logdecay.shape[-1]
    place = jnp.arange(length)
    lower = place[:, None] >= place[None, :]
    upper = place[:, None] <= place[None, :]
    later = running[..., :, None] - running[..., None, :]
    shifted = running - logdecay
    earlier = shifted[..., None, :] - shifted[..., :, None]
    forward = jnp.exp(jnp.where(lower, later, -jnp.inf))
    backward = jnp.exp(jnp.where(upper, earlier, -jnp.inf))
    return forward + backward


def scan_grid(values, maps, logdecay, along_rows):
    heads = logdecay.shape[-1]
    in_map = maps[..., :STATE]
    out_map = maps[..., STATE:]
    split_values = values.reshape(values.shape[:3] + (heads, HEAD_DIM))
    if along_rows:
        scores = jnp.einsum("ialn,iamn->ialm", out_map, in_map, preferred_element_type=jnp.float32)
        decays = jnp.moveaxis(logdecay.astype(jnp.float32), 3, 2)
    else:
        scores = jnp.einsum("ilan,iman->ialm", out_map, in_map, preferred_element_type=jnp.float32)
        decays = jnp.transpose(logdecay.astype(jnp.float32), (0, 2, 3, 1))
    weights = (scores[:, :, None] * kernel(decays)).astype(jnp.bfloat16)
    if along_rows:
        result = jnp.einsum(
            "iahlm,iamhp->ialhp", weights, split_values, preferred_element_type=jnp.float32
        )
    else:
        result = jnp.einsum(
            "iahlm,imahp->ilahp", weights, split_values, preferred_element_type=jnp.float32
        )
    return result.reshape(values.shape)


def on_device(
    tokens, in_gain, w_inner, w_bc, w_step, step_bias, decay_rate, skip, norm_gain, w_out
):
    whole = lax.all_gather(tokens.astype(jnp.bfloat16), "tensor", axis=3, tiled=True)
    rounded = whole.astype(jnp.float32)
    scale = lax.rsqrt(jnp.mean(rounded * rounded, axis=-1, keepdims=True) + EPS)
    normed = (rounded * scale * in_gain).astype(jnp.bfloat16)
    inner = jnp.einsum("irwd,dc->irwc", normed, w_inner, preferred_element_type=jnp.float32).astype(
        jnp.bfloat16
    )
    maps = jnp.einsum("irwd,dc->irwc", normed, w_bc, preferred_element_type=jnp.float32).astype(
        jnp.bfloat16
    )
    step = jax.nn.softplus(
        jnp.einsum("irwd,dc->irwc", normed, w_step, preferred_element_type=jnp.float32) + step_bias
    )
    logdecay = (-decay_rate * step).astype(jnp.bfloat16)
    heads_local = w_step.shape[1]
    lead = inner.shape[:3]
    value = (
        (inner.reshape(lead + (heads_local, HEAD_DIM)).astype(jnp.float32) * step[..., None])
        .reshape(inner.shape)
        .astype(jnp.bfloat16)
    )
    share = maps.shape[3] // lax.axis_size("tensor")
    maps_sent = lax.dynamic_slice_in_dim(maps, lax.axis_index("tensor") * share, share, 3)
    col_value = lax.all_to_all(value, "space", split_axis=2, concat_axis=1, tiled=True)
    col_maps = lax.all_to_all(maps_sent, "space", split_axis=2, concat_axis=1, tiled=True)
    col_decay = lax.all_to_all(logdecay, "space", split_axis=2, concat_axis=1, tiled=True)
    col_maps = lax.all_gather(col_maps, "tensor", axis=3, tiled=True)
    column_out = scan_grid(col_value, col_maps, col_decay, False).astype(jnp.bfloat16)
    column_back = lax.all_to_all(column_out, "space", split_axis=1, concat_axis=2, tiled=True)
    row_out = scan_grid(value, maps, logdecay, True)
    skip_wide = jnp.repeat(skip, HEAD_DIM)
    total = row_out + column_back.astype(jnp.float32) + skip_wide * inner.astype(jnp.float32)
    group = NORM_HEADS * HEAD_DIM
    grouped = total.reshape(lead + (inner.shape[3] // group, group))
    norm_scale = lax.rsqrt(jnp.mean(grouped * grouped, axis=-1, keepdims=True) + EPS)
    gated = ((grouped * norm_scale).reshape(inner.shape) * norm_gain).astype(jnp.bfloat16)
    partial_out = jnp.einsum("irwc,cd->irwd", gated, w_out, preferred_element_type=jnp.float32)
    mixer = lax.psum_scatter(partial_out, "tensor", scatter_dimension=3, tiled=True)
    return (tokens + mixer).astype(jnp.bfloat16)


LANES = 128
SUBLANES = 8
LOG2E = 1.4426950408889634
PARTS = 4
VMEM_LIMIT = 60 * 1024 * 1024


def params(**extra):
    return pltpu.CompilerParams(vmem_limit_bytes=VMEM_LIMIT, **extra)


def resident(shape, index_map):
    return pl.BlockSpec(shape, index_map, pipeline_mode=pl.Buffered(1))


def turn_kernel(rows, tok_ref, out_ref, held):
    width = tok_ref.shape[2]
    for lane in range(tok_ref.shape[3] // LANES):
        part = slice(lane * LANES, (lane + 1) * LANES)
        for row in range(rows):
            held[lane, pl.ds(row, width, stride=rows), :] = tok_ref[0, row, :, part]
        out_ref[:, part] = held[lane].astype(jnp.bfloat16)


def turn(tokens, start, count):
    _, rows, columns, feats = tokens.shape
    step = columns // PARTS
    return pl.pallas_call(
        functools.partial(turn_kernel, rows),
        grid=(count,),
        in_specs=[grid_block(tokens, start)],
        out_specs=pl.BlockSpec((step * rows, feats), lambda k: (k, 0)),
        out_shape=jax.ShapeDtypeStruct((count * step * rows, feats), jnp.bfloat16),
        scratch_shapes=[pltpu.VMEM((feats // LANES, step * rows, LANES), jnp.float32)],
        compiler_params=params(),
        cost_estimate=pl.CostEstimate(
            flops=0, transcendentals=0, bytes_accessed=6 * count * step * rows * feats
        ),
        name="turn",
    )(tokens)


def grid_block(tokens, start):
    _, rows, columns, feats = tokens.shape

    def place(k):
        at = start + k
        return at // PARTS, 0, at % PARTS, 0

    return pl.BlockSpec((1, rows, columns // PARTS, feats), place)


def project_kernel(
    depth, heads, t_ref, own_ref, other_ref, g_own, g_other, w_own, w_other, m_own, m_other,
    bias_ref, rate_ref, *rest,
):
    inner_ref, pack_ref = rest[-2:]
    own = own_ref[...].astype(jnp.float32)
    other = other_ref[...].astype(jnp.float32)
    squares = jnp.sum(own * own, axis=-1, keepdims=True) + jnp.sum(
        other * other, axis=-1, keepdims=True
    )
    scale = lax.rsqrt(squares / depth + EPS)
    n_own = (own * scale * g_own[0]).astype(jnp.bfloat16)
    n_other = (other * scale * g_other[0]).astype(jnp.bfloat16)

    def project(a, b):
        return jnp.dot(n_own, a, preferred_element_type=jnp.float32) + jnp.dot(
            n_other, b, preferred_element_type=jnp.float32
        )

    small = project(m_own[0], m_other[0])
    wide = inner_ref.shape[1]
    step = jax.nn.softplus(small[:, 2 * STATE :] + bias_ref[...])
    blocks = pack_ref.shape[:2]

    def put(start, block):
        lanes = block.shape[1]
        pack_ref[:, :, start : start + lanes] = block.astype(jnp.bfloat16).reshape(blocks + (lanes,))

    put(wide, small[:, : 2 * STATE])
    put(wide + 2 * STATE, -rate_ref[...] * step)
    inner = project(w_own[0], w_other[0]).astype(jnp.bfloat16)
    inner_ref[...] = inner
    rows = inner.shape[0]
    low = lax.broadcasted_iota(jnp.int32, (rows, LANES), 1) < HEAD_DIM
    for pair in range(heads // 2):
        part = slice(pair * LANES, (pair + 1) * LANES)
        spread = jnp.where(
            low, step[:, 2 * pair : 2 * pair + 1], step[:, 2 * pair + 1 : 2 * pair + 2]
        )
        put(pair * LANES, inner[:, part].astype(jnp.float32) * spread)


def project(own, other, in_gain, w_inner, w_small, bias, rate, place, heads, owners, start, count, total, earlier):
    rows, feats = own.shape
    wide = w_inner.shape[1]
    small = w_small.shape[1]
    tile = rows // count
    depth = tile // owners
    chained = [] if earlier is None else [earlier]
    gains = in_gain.reshape(2, 1, feats)
    w_inner = w_inner.reshape(2, feats, wide)
    w_small = w_small.reshape(2, feats, small)
    row_spec = pl.BlockSpec((tile, feats), lambda i, t: (i, 0))

    def pair(shape):
        return [
            resident((1,) + shape, lambda i, t: (t[0], 0, 0)),
            resident((1,) + shape, lambda i, t: (1 - t[0], 0, 0)),
        ]

    packed = wide + small
    return pl.pallas_call(
        functools.partial(project_kernel, 2 * feats, heads),
        grid_spec=pltpu.PrefetchScalarGridSpec(
            num_scalar_prefetch=1,
            grid=(rows // tile,),
            in_specs=[row_spec, row_spec]
            + pair((1, feats))
            + pair((feats, wide))
            + pair((feats, small))
            + [resident((1, LANES), lambda i, t: (0, 0))] * 2
            + [pl.BlockSpec(memory_space=pl.ANY)] * len(chained),
            out_specs=[
                pl.BlockSpec((tile, wide), lambda i, t: (start + i, 0)),
                pl.BlockSpec((owners, depth, packed), lambda i, t: (0, i, 0)),
            ],
        ),
        out_shape=[
            jax.ShapeDtypeStruct((total * tile, wide), jnp.bfloat16),
            jax.ShapeDtypeStruct((owners, count * depth, packed), jnp.bfloat16),
        ],
        input_output_aliases={11: 0} if chained else {},
        compiler_params=params(),
        cost_estimate=pl.CostEstimate(
            flops=4 * rows * feats * packed, transcendentals=0, bytes_accessed=20 * 2**20
        ),
        name="project",
    )(place, own, other, gains, gains, w_inner, w_inner, w_small, w_small, bias, rate, *chained)


def scan_sequence(length, heads, in_map, out_map, decay, value_of, store):
    row = lax.broadcasted_iota(jnp.int32, (length, length), 0)
    col = lax.broadcasted_iota(jnp.int32, (length, length), 1)
    lower = row >= col
    ones = jnp.where(lower, 1.0, 0.0).astype(jnp.bfloat16)
    eye = jnp.where(row == col, 1.0, 0.0).astype(jnp.bfloat16)
    scores = lax.dot_general(
        out_map, in_map, (((1,), (1,)), ((), ())), preferred_element_type=jnp.float32
    )
    scores = jnp.where(row == col, scores + scores, scores)
    running = jnp.dot(ones, decay, preferred_element_type=jnp.float32) * LOG2E
    shifted = running - decay.astype(jnp.float32) * LOG2E
    turned = lax.dot_general(
        decay, ones, (((0,), (1,)), ((), ())), preferred_element_type=jnp.float32
    )
    turned_decay = lax.dot_general(
        decay, eye, (((0,), (1,)), ((), ())), preferred_element_type=jnp.float32
    )
    running_row = turned * LOG2E
    shifted_row = running_row - turned_decay * LOG2E
    low = lax.broadcasted_iota(jnp.int32, (length, LANES), 1) < HEAD_DIM
    for pair in range(heads // 2):
        weights = []
        for head in (2 * pair, 2 * pair + 1):
            later = running[:, head : head + 1] - running_row[head : head + 1, :]
            earlier = shifted_row[head : head + 1, :] - shifted[:, head : head + 1]
            decayed = jnp.exp2(jnp.where(lower, later, earlier))
            weights.append((scores * decayed).astype(jnp.bfloat16))
        value = value_of(pair)
        zero = jnp.zeros_like(value)
        stacked = jnp.concatenate(
            [jnp.where(low, value, zero), jnp.where(low, zero, value)], axis=0
        ).astype(jnp.bfloat16)
        store(
            pair,
            jnp.dot(
                jnp.concatenate(weights, axis=1), stacked, preferred_element_type=jnp.float32
            ),
        )


def column_kernel(heads, pack_ref, *rest):
    out_ref = rest[-1]
    owners, _, rows, _ = pack_ref.shape
    length = owners * rows
    wide = out_ref.shape[3]

    def take(start):
        block = pack_ref[:, 0, :, start : start + LANES].astype(jnp.float32)
        return block.reshape(length, LANES)

    def store(pair, result):
        out_ref[:, 0, :, pair * LANES : (pair + 1) * LANES] = result.reshape(
            owners, rows, LANES
        ).astype(jnp.bfloat16)

    scan_sequence(
        length,
        heads,
        take(wide).astype(jnp.bfloat16),
        take(wide + STATE).astype(jnp.bfloat16),
        take(wide + 2 * STATE).astype(jnp.bfloat16),
        lambda pair: take(pair * LANES),
        store,
    )


def scan_cost(sequences, length, heads):
    return pl.CostEstimate(
        flops=8 * sequences * heads * length * length * LANES,
        transcendentals=sequences * heads * length * length,
        bytes_accessed=sequences * length * heads * HEAD_DIM * 6,
    )


def column_scan(pack, heads, first, count, offset, total, earlier):
    owners, _, rows, packed = pack.shape
    wide = heads * HEAD_DIM
    chained = [] if earlier is None else [earlier]
    return pl.pallas_call(
        functools.partial(column_kernel, heads),
        grid=(count,),
        in_specs=[pl.BlockSpec((owners, 1, rows, packed), lambda c: (0, first + c, 0, 0))]
        + [pl.BlockSpec(memory_space=pl.ANY)] * len(chained),
        out_specs=pl.BlockSpec((owners, 1, rows, wide), lambda c: (0, offset + c, 0, 0)),
        out_shape=jax.ShapeDtypeStruct((owners, total, rows, wide), jnp.bfloat16),
        input_output_aliases={1: 0} if chained else {},
        compiler_params=params(),
        cost_estimate=scan_cost(count, owners * rows, heads),
        name="column_scan",
    )(pack, *chained)


def row_kernel(rows, heads, counts, *refs):
    packs, out_ref, held = refs[:-2], refs[-2], refs[-1]
    image, row = pl.program_id(0), pl.program_id(1)
    wide = heads * HEAD_DIM
    tall = held.shape[1] // PARTS
    length = held.shape[1] // rows
    units = [(pack, k) for pack, count in zip(packs, counts) for k in range(count)]

    for u, (pack, k) in enumerate(units):

        @pl.when((row == 0) & (image == u // PARTS))
        def _(pack=pack, k=k, part=u % PARTS):
            depth = tall // pack.shape[0]
            for lane in range(pack.shape[2] // LANES):
                block = pack[:, k * depth : (k + 1) * depth, lane * LANES : (lane + 1) * LANES]
                held[lane, part * tall : (part + 1) * tall, :] = block.reshape(
                    tall, LANES
                ).astype(jnp.float32)

    def take(lane):
        return held[lane, pl.ds(row, length, stride=rows), :]

    def store(pair, result):
        out_ref[pair, pl.ds(row, length, stride=rows), :] = result

    first = wide // LANES
    scan_sequence(
        length,
        heads,
        take(first).astype(jnp.bfloat16),
        take(first + 1).astype(jnp.bfloat16),
        take(first + 2).astype(jnp.bfloat16),
        take,
        store,
    )


def row_scan(packs, counts, images, rows, columns, heads):
    packed = packs[0].shape[2]
    total = rows * columns
    wide = heads * HEAD_DIM
    return pl.pallas_call(
        functools.partial(row_kernel, rows, heads, counts),
        grid=(images, rows),
        in_specs=[resident(pack.shape, lambda i, r: (0, 0, 0)) for pack in packs],
        out_specs=pl.BlockSpec((wide // LANES, total, LANES), lambda i, r: (0, i, 0)),
        out_shape=jax.ShapeDtypeStruct((wide // LANES, images * total, LANES), jnp.float32),
        scratch_shapes=[pltpu.VMEM((packed // LANES, total, LANES), jnp.float32)],
        compiler_params=params(),
        cost_estimate=scan_cost(images * rows, columns, heads),
        name="row_scan",
    )(*packs)


def output_kernel(t_ref, row_ref, col_ref, inner_ref, skip_ref, gain_ref, w_own, w_other, own_ref, send_ref):
    tall, wide = inner_ref.shape
    group = NORM_HEADS * HEAD_DIM
    gated = []
    for start in range(0, wide, group):
        parts = []
        squares = 0.0
        for lane in range(start, start + group, LANES):
            part = slice(lane, lane + LANES)
            total = (
                row_ref[lane // LANES]
                + col_ref[:, :, part].astype(jnp.float32).reshape(tall, LANES)
                + skip_ref[:, part] * inner_ref[:, part].astype(jnp.float32)
            )
            parts.append(total)
            squares = squares + total * total
        scale = lax.rsqrt(jnp.sum(squares, axis=-1, keepdims=True) / group + EPS)
        for k, total in enumerate(parts):
            lane = start + k * LANES
            gated.append((total * scale * gain_ref[:, lane : lane + LANES]).astype(jnp.bfloat16))
    gated = jnp.concatenate(gated, axis=1)
    send_ref[...] = jnp.dot(gated, w_other[...], preferred_element_type=jnp.float32).astype(
        jnp.bfloat16
    )
    own_ref[...] = jnp.dot(gated, w_own[...], preferred_element_type=jnp.float32)


def output(row_out, start, count, col, inner, skip, gain, w_out, place):
    wide = inner.shape[1]
    feats = w_out.shape[1] // 2
    depth = col.shape[1] // count
    owners = col.shape[0]
    tile = owners * depth
    rows = tile * count
    row_spec = pl.BlockSpec((tile, wide), lambda i, t: (start + i, 0))
    out_spec = pl.BlockSpec((tile, feats), lambda i, t: (i, 0))
    return pl.pallas_call(
        output_kernel,
        grid_spec=pltpu.PrefetchScalarGridSpec(
            num_scalar_prefetch=1,
            grid=(count,),
            in_specs=[
                pl.BlockSpec((wide // LANES, tile, LANES), lambda i, t: (0, start + i, 0)),
                pl.BlockSpec((owners, depth, wide), lambda i, t: (0, i, 0)),
                row_spec,
                resident((1, wide), lambda i, t: (0, 0)),
                resident((1, wide), lambda i, t: (0, 0)),
                resident((wide, feats), lambda i, t: (0, t[0])),
                resident((wide, feats), lambda i, t: (0, 1 - t[0])),
            ],
            out_specs=[out_spec, out_spec],
        ),
        out_shape=[
            jax.ShapeDtypeStruct((rows, feats), jnp.float32),
            jax.ShapeDtypeStruct((rows, feats), jnp.bfloat16),
        ],
        compiler_params=params(),
        cost_estimate=pl.CostEstimate(
            flops=4 * rows * feats * wide, transcendentals=0, bytes_accessed=16 * 2**20
        ),
        name="output",
    )(place, row_out, col, inner, skip, gain, w_out, w_out)


def finish_kernel(rows, own_ref, got_ref, tok_ref, *rest):
    out_ref, held = rest[-2:]
    width = tok_ref.shape[2]
    for lane in range(tok_ref.shape[3] // LANES):
        part = slice(lane * LANES, (lane + 1) * LANES)
        held[lane] = own_ref[:, part] + got_ref[:, part].astype(jnp.float32)
        for row in range(rows):
            out_ref[0, row, :, part] = (
                tok_ref[0, row, :, part] + held[lane, pl.ds(row, width, stride=rows), :]
            ).astype(jnp.bfloat16)


def finish(own, got, tokens, start, count, earlier):
    _, rows, columns, feats = tokens.shape
    step = columns // PARTS
    flat = pl.BlockSpec((step * rows, feats), lambda k: (k, 0))
    chained = [] if earlier is None else [earlier]
    return pl.pallas_call(
        functools.partial(finish_kernel, rows),
        grid=(count,),
        in_specs=[flat, flat, grid_block(tokens, start)]
        + [pl.BlockSpec(memory_space=pl.ANY)] * len(chained),
        out_specs=grid_block(tokens, start),
        out_shape=jax.ShapeDtypeStruct(tokens.shape, jnp.bfloat16),
        scratch_shapes=[pltpu.VMEM((feats // LANES, step * rows, LANES), jnp.float32)],
        input_output_aliases={3: 0} if chained else {},
        compiler_params=params(),
        cost_estimate=pl.CostEstimate(
            flops=0, transcendentals=0, bytes_accessed=12 * count * step * rows * feats
        ),
        name="finish",
    )(own, got, tokens, *chained)


def pipelined(
    owners, tokens, in_gain, w_inner, w_bc, w_step, step_bias, decay_rate, skip, norm_gain, w_out
):
    images, rows, columns, _ = tokens.shape
    heads = w_step.shape[1]
    wide = w_inner.shape[1]
    swap = [(0, 1), (1, 0)]
    place = lax.axis_index("tensor").astype(jnp.int32).reshape(1)
    pad = LANES - heads
    w_small = jnp.concatenate([w_bc, jnp.pad(w_step, ((0, 0), (0, pad)))], axis=1)
    bias = jnp.pad(step_bias, (0, pad)).reshape(1, LANES)
    rate = jnp.pad(decay_rate, (0, pad)).reshape(1, LANES)
    skip_wide = jnp.repeat(skip, HEAD_DIM).reshape(1, wide)
    gain = norm_gain.reshape(1, wide)
    units = images * PARTS
    per_unit = columns // PARTS // owners
    there = groups_of((1, units // 2 - 1, units - units // 2))
    back = groups_of((units // 2, units // 4, units - units // 2 - units // 4))
    own, other, packs, arrived = [], [], [], []
    for start, count in there:
        own.append(turn(tokens, start, count))
    for g in range(len(there)):
        other.append(lax.ppermute(own[g], "tensor", swap))
    inner = None
    for g, (start, count) in enumerate(there):
        inner, pack = project(
            own[g], other[g], in_gain, w_inner, w_small, bias, rate, place, heads, owners,
            start, count, units, inner,
        )
        packs.append(pack)
        block = lax.all_to_all(pack, "space", split_axis=0, concat_axis=0, tiled=True)
        arrived.append(block.reshape(owners, count * per_unit, rows, pack.shape[2]))
    counts = tuple(count for _, count in there)
    row_out = row_scan(packs, counts, images, rows, columns, heads)
    columns_out = [None] * len(back)
    for g, (start, count) in enumerate(there):
        for k, (low, size) in enumerate(back):
            first, last = max(start, low), min(start + count, low + size)
            if first < last:
                columns_out[k] = column_scan(
                    arrived[g], heads, (first - start) * per_unit, (last - first) * per_unit,
                    (first - low) * per_unit, size * per_unit, columns_out[k],
                )
    result = None
    for k, (start, count) in enumerate(back):
        block = columns_out[k].reshape(owners, count * per_unit * rows, wide)
        block = lax.all_to_all(block, "space", split_axis=0, concat_axis=0, tiled=True)
        kept, send = output(row_out, start, count, block, inner, skip_wide, gain, w_out, place)
        got = lax.ppermute(send, "tensor", swap)
        result = finish(kept, got, tokens, start, count, result)
    return result


def groups_of(counts):
    starts = [sum(counts[:k]) for k in range(len(counts))]
    return list(zip(starts, counts))


def fits(owners, tensor, tokens, heads):
    images, rows, columns, _ = tokens
    return (
        tensor == 2
        and images * PARTS == 8
        and rows == SUBLANES
        and columns % (PARTS * owners) == 0
        and owners * rows == columns == LANES
        and heads % NORM_HEADS == 0
        and heads % 2 == 0
        and heads <= LANES
        and STATE == LANES == 2 * HEAD_DIM
    )


def dispatch(owners, tensor, tokens, *rest):
    if fits(owners, tensor, tokens.shape, rest[3].shape[1]):
        return pipelined(owners, tokens, *rest)
    return on_device(tokens, *rest)


def solution(mesh):
    body = functools.partial(dispatch, mesh.shape["space"], mesh.shape["tensor"])
    return jax.shard_map(
        body,
        mesh=mesh,
        in_specs=(
            P(None, "space", None, "tensor"),
            P(),
            P(None, "tensor"),
            P(),
            P(None, "tensor"),
            P("tensor"),
            P("tensor"),
            P("tensor"),
            P("tensor"),
            P("tensor", None),
        ),
        out_specs=P(None, "space", None, "tensor"),
        check_vma=False,
    )
```

```python
import functools

import jax
import jax.numpy as jnp
from jax import lax
from jax.experimental import pallas as pl
from jax.experimental.pallas import tpu as pltpu
from jax.sharding import PartitionSpec as P

HEAD_DIM = 64
STATE = 128
NORM_HEADS = 6


EPS = 1e-05


def kernel(logdecay):
    running = jnp.cumsum(logdecay, axis=-1)
    length = logdecay.shape[-1]
    place = jnp.arange(length)
    lower = place[:, None] >= place[None, :]
    upper = place[:, None] <= place[None, :]
    later = running[..., :, None] - running[..., None, :]
    shifted = running - logdecay
    earlier = shifted[..., None, :] - shifted[..., :, None]
    forward = jnp.exp(jnp.where(lower, later, -jnp.inf))
    backward = jnp.exp(jnp.where(upper, earlier, -jnp.inf))
    return forward + backward


def scan_grid(values, maps, logdecay, along_rows):
    heads = logdecay.shape[-1]
    in_map = maps[..., :STATE]
    out_map = maps[..., STATE:]
    split_values = values.reshape(values.shape[:3] + (heads, HEAD_DIM))
    if along_rows:
        scores = jnp.einsum("ialn,iamn->ialm", out_map, in_map, preferred_element_type=jnp.float32)
        decays = jnp.moveaxis(logdecay.astype(jnp.float32), 3, 2)
    else:
        scores = jnp.einsum("ilan,iman->ialm", out_map, in_map, preferred_element_type=jnp.float32)
        decays = jnp.transpose(logdecay.astype(jnp.float32), (0, 2, 3, 1))
    weights = (scores[:, :, None] * kernel(decays)).astype(jnp.bfloat16)
    if along_rows:
        result = jnp.einsum(
            "iahlm,iamhp->ialhp", weights, split_values, preferred_element_type=jnp.float32
        )
    else:
        result = jnp.einsum(
            "iahlm,imahp->ilahp", weights, split_values, preferred_element_type=jnp.float32
        )
    return result.reshape(values.shape)


def on_device(
    tokens, in_gain, w_inner, w_bc, w_step, step_bias, decay_rate, skip, norm_gain, w_out
):
    whole = lax.all_gather(tokens.astype(jnp.bfloat16), "tensor", axis=3, tiled=True)
    rounded = whole.astype(jnp.float32)
    scale = lax.rsqrt(jnp.mean(rounded * rounded, axis=-1, keepdims=True) + EPS)
    normed = (rounded * scale * in_gain).astype(jnp.bfloat16)
    inner = jnp.einsum("irwd,dc->irwc", normed, w_inner, preferred_element_type=jnp.float32).astype(
        jnp.bfloat16
    )
    maps = jnp.einsum("irwd,dc->irwc", normed, w_bc, preferred_element_type=jnp.float32).astype(
        jnp.bfloat16
    )
    step = jax.nn.softplus(
        jnp.einsum("irwd,dc->irwc", normed, w_step, preferred_element_type=jnp.float32) + step_bias
    )
    logdecay = (-decay_rate * step).astype(jnp.bfloat16)
    heads_local = w_step.shape[1]
    lead = inner.shape[:3]
    value = (
        (inner.reshape(lead + (heads_local, HEAD_DIM)).astype(jnp.float32) * step[..., None])
        .reshape(inner.shape)
        .astype(jnp.bfloat16)
    )
    share = maps.shape[3] // lax.axis_size("tensor")
    maps_sent = lax.dynamic_slice_in_dim(maps, lax.axis_index("tensor") * share, share, 3)
    col_value = lax.all_to_all(value, "space", split_axis=2, concat_axis=1, tiled=True)
    col_maps = lax.all_to_all(maps_sent, "space", split_axis=2, concat_axis=1, tiled=True)
    col_decay = lax.all_to_all(logdecay, "space", split_axis=2, concat_axis=1, tiled=True)
    col_maps = lax.all_gather(col_maps, "tensor", axis=3, tiled=True)
    column_out = scan_grid(col_value, col_maps, col_decay, False).astype(jnp.bfloat16)
    column_back = lax.all_to_all(column_out, "space", split_axis=1, concat_axis=2, tiled=True)
    row_out = scan_grid(value, maps, logdecay, True)
    skip_wide = jnp.repeat(skip, HEAD_DIM)
    total = row_out + column_back.astype(jnp.float32) + skip_wide * inner.astype(jnp.float32)
    group = NORM_HEADS * HEAD_DIM
    grouped = total.reshape(lead + (inner.shape[3] // group, group))
    norm_scale = lax.rsqrt(jnp.mean(grouped * grouped, axis=-1, keepdims=True) + EPS)
    gated = ((grouped * norm_scale).reshape(inner.shape) * norm_gain).astype(jnp.bfloat16)
    partial_out = jnp.einsum("irwc,cd->irwd", gated, w_out, preferred_element_type=jnp.float32)
    mixer = lax.psum_scatter(partial_out, "tensor", scatter_dimension=3, tiled=True)
    return (tokens + mixer).astype(jnp.bfloat16)


LANES = 128
SUBLANES = 8
LOG2E = 1.4426950408889634
PARTS = 4
VMEM_LIMIT = 60 * 1024 * 1024


def params(**extra):
    return pltpu.CompilerParams(vmem_limit_bytes=VMEM_LIMIT, **extra)


def resident(shape, index_map):
    return pl.BlockSpec(shape, index_map, pipeline_mode=pl.Buffered(1))


def turn_kernel(rows, tok_ref, out_ref, held):
    width = tok_ref.shape[2]
    for lane in range(tok_ref.shape[3] // LANES):
        part = slice(lane * LANES, (lane + 1) * LANES)
        for row in range(rows):
            held[lane, pl.ds(row, width, stride=rows), :] = tok_ref[0, row, :, part]
        out_ref[:, part] = held[lane].astype(jnp.bfloat16)


def turn(tokens, start, count):
    _, rows, columns, feats = tokens.shape
    step = columns // PARTS
    return pl.pallas_call(
        functools.partial(turn_kernel, rows),
        grid=(count,),
        in_specs=[grid_block(tokens, start)],
        out_specs=pl.BlockSpec((step * rows, feats), lambda k: (k, 0)),
        out_shape=jax.ShapeDtypeStruct((count * step * rows, feats), jnp.bfloat16),
        scratch_shapes=[pltpu.VMEM((feats // LANES, step * rows, LANES), jnp.float32)],
        compiler_params=params(),
        cost_estimate=pl.CostEstimate(
            flops=0, transcendentals=0, bytes_accessed=6 * count * step * rows * feats
        ),
        name="turn",
    )(tokens)


def grid_block(tokens, start):
    _, rows, columns, feats = tokens.shape

    def place(k):
        at = start + k
        return at // PARTS, 0, at % PARTS, 0

    return pl.BlockSpec((1, rows, columns // PARTS, feats), place)


def project_kernel(
    depth, heads, t_ref, own_ref, other_ref, g_own, g_other, w_own, w_other, m_own, m_other,
    bias_ref, rate_ref, *rest,
):
    inner_ref, pack_ref, spare_ref = rest[-3:]
    own = own_ref[...].astype(jnp.float32)
    other = other_ref[...].astype(jnp.float32)
    squares = jnp.sum(own * own, axis=-1, keepdims=True) + jnp.sum(
        other * other, axis=-1, keepdims=True
    )
    scale = lax.rsqrt(squares / depth + EPS)
    n_own = (own * scale * g_own[0]).astype(jnp.bfloat16)
    n_other = (other * scale * g_other[0]).astype(jnp.bfloat16)

    def project(a, b):
        return jnp.dot(n_own, a, preferred_element_type=jnp.float32) + jnp.dot(
            n_other, b, preferred_element_type=jnp.float32
        )

    small = project(m_own[0], m_other[0])
    wide = inner_ref.shape[1]
    step = jax.nn.softplus(small[:, 2 * STATE :] + bias_ref[...])
    blocks = pack_ref.shape[:2]

    def put(start, block):
        lanes = block.shape[1]
        pack_ref[:, :, start : start + lanes] = block.astype(jnp.bfloat16).reshape(blocks + (lanes,))

    first = t_ref[0] == 0
    in_map, out_map = small[:, :STATE], small[:, STATE : 2 * STATE]
    put(wide, jnp.where(first, in_map, out_map))
    put(wide + STATE, -rate_ref[...] * step)
    spare_ref[...] = (
        jnp.where(first, out_map, in_map).astype(jnp.bfloat16).reshape(spare_ref.shape)
    )
    inner = project(w_own[0], w_other[0]).astype(jnp.bfloat16)
    inner_ref[...] = inner
    rows = inner.shape[0]
    low = lax.broadcasted_iota(jnp.int32, (rows, LANES), 1) < HEAD_DIM
    for pair in range(heads // 2):
        part = slice(pair * LANES, (pair + 1) * LANES)
        spread = jnp.where(
            low, step[:, 2 * pair : 2 * pair + 1], step[:, 2 * pair + 1 : 2 * pair + 2]
        )
        put(pair * LANES, inner[:, part].astype(jnp.float32) * spread)


def project(own, other, in_gain, w_inner, w_small, bias, rate, place, heads, owners, start, count, total, earlier):
    rows, feats = own.shape
    wide = w_inner.shape[1]
    small = w_small.shape[1]
    tile = rows // count
    depth = tile // owners
    chained = [] if earlier is None else [earlier]
    gains = in_gain.reshape(2, 1, feats)
    w_inner = w_inner.reshape(2, feats, wide)
    w_small = w_small.reshape(2, feats, small)
    row_spec = pl.BlockSpec((tile, feats), lambda i, t: (i, 0))

    def pair(shape):
        return [
            resident((1,) + shape, lambda i, t: (t[0], 0, 0)),
            resident((1,) + shape, lambda i, t: (1 - t[0], 0, 0)),
        ]

    packed = wide + small - STATE
    return pl.pallas_call(
        functools.partial(project_kernel, 2 * feats, heads),
        grid_spec=pltpu.PrefetchScalarGridSpec(
            num_scalar_prefetch=1,
            grid=(rows // tile,),
            in_specs=[row_spec, row_spec]
            + pair((1, feats))
            + pair((feats, wide))
            + pair((feats, small))
            + [resident((1, LANES), lambda i, t: (0, 0))] * 2
            + [pl.BlockSpec(memory_space=pl.ANY)] * len(chained),
            out_specs=[
                pl.BlockSpec((tile, wide), lambda i, t: (start + i, 0)),
                pl.BlockSpec((owners, depth, packed), lambda i, t: (0, i, 0)),
                pl.BlockSpec((owners, depth, STATE), lambda i, t: (0, i, 0)),
            ],
        ),
        out_shape=[
            jax.ShapeDtypeStruct((total * tile, wide), jnp.bfloat16),
            jax.ShapeDtypeStruct((owners, count * depth, packed), jnp.bfloat16),
            jax.ShapeDtypeStruct((owners, count * depth, STATE), jnp.bfloat16),
        ],
        input_output_aliases={11: 0} if chained else {},
        compiler_params=params(),
        cost_estimate=pl.CostEstimate(
            flops=4 * rows * feats * packed, transcendentals=0, bytes_accessed=20 * 2**20
        ),
        name="project",
    )(place, own, other, gains, gains, w_inner, w_inner, w_small, w_small, bias, rate, *chained)


def scan_sequence(length, heads, in_map, out_map, decay, value_of, store):
    row = lax.broadcasted_iota(jnp.int32, (length, length), 0)
    col = lax.broadcasted_iota(jnp.int32, (length, length), 1)
    lower = row >= col
    ones = jnp.where(lower, 1.0, 0.0).astype(jnp.bfloat16)
    eye = jnp.where(row == col, 1.0, 0.0).astype(jnp.bfloat16)
    scores = lax.dot_general(
        out_map, in_map, (((1,), (1,)), ((), ())), preferred_element_type=jnp.float32
    )
    scores = jnp.where(row == col, scores + scores, scores)
    running = jnp.dot(ones, decay, preferred_element_type=jnp.float32) * LOG2E
    shifted = running - decay.astype(jnp.float32) * LOG2E
    turned = lax.dot_general(
        decay, ones, (((0,), (1,)), ((), ())), preferred_element_type=jnp.float32
    )
    turned_decay = lax.dot_general(
        decay, eye, (((0,), (1,)), ((), ())), preferred_element_type=jnp.float32
    )
    running_row = turned * LOG2E
    shifted_row = running_row - turned_decay * LOG2E
    low = lax.broadcasted_iota(jnp.int32, (length, LANES), 1) < HEAD_DIM
    for pair in range(heads // 2):
        weights = []
        for head in (2 * pair, 2 * pair + 1):
            later = running[:, head : head + 1] - running_row[head : head + 1, :]
            earlier = shifted_row[head : head + 1, :] - shifted[:, head : head + 1]
            decayed = jnp.exp2(jnp.where(lower, later, earlier))
            weights.append((scores * decayed).astype(jnp.bfloat16))
        value = value_of(pair)
        zero = jnp.zeros_like(value)
        stacked = jnp.concatenate(
            [jnp.where(low, value, zero), jnp.where(low, zero, value)], axis=0
        ).astype(jnp.bfloat16)
        store(
            pair,
            jnp.dot(
                jnp.concatenate(weights, axis=1), stacked, preferred_element_type=jnp.float32
            ),
        )


def both_maps(mine, spare):
    first = lax.axis_index("tensor") == 0
    in_map = jnp.where(first, mine, spare).astype(jnp.bfloat16)
    out_map = jnp.where(first, spare, mine).astype(jnp.bfloat16)
    return in_map, out_map


def column_kernel(heads, pack_ref, spare_ref, *rest):
    out_ref = rest[-1]
    owners, _, rows, _ = pack_ref.shape
    length = owners * rows
    wide = out_ref.shape[3]

    def take(start):
        block = pack_ref[:, 0, :, start : start + LANES].astype(jnp.float32)
        return block.reshape(length, LANES)

    def store(pair, result):
        out_ref[:, 0, :, pair * LANES : (pair + 1) * LANES] = result.reshape(
            owners, rows, LANES
        ).astype(jnp.bfloat16)

    scan_sequence(
        length,
        heads,
        *both_maps(take(wide), spare_ref[:, 0, :, :].astype(jnp.float32).reshape(length, STATE)),
        take(wide + STATE).astype(jnp.bfloat16),
        lambda pair: take(pair * LANES),
        store,
    )


def scan_cost(sequences, length, heads):
    return pl.CostEstimate(
        flops=8 * sequences * heads * length * length * LANES,
        transcendentals=sequences * heads * length * length,
        bytes_accessed=sequences * length * heads * HEAD_DIM * 6,
    )


def column_scan(pack, spare, heads, first, count, offset, total, earlier):
    owners, _, rows, packed = pack.shape
    wide = heads * HEAD_DIM
    chained = [] if earlier is None else [earlier]
    return pl.pallas_call(
        functools.partial(column_kernel, heads),
        grid=(count,),
        in_specs=[
            pl.BlockSpec((owners, 1, rows, packed), lambda c: (0, first + c, 0, 0)),
            pl.BlockSpec((owners, 1, rows, STATE), lambda c: (0, first + c, 0, 0)),
        ]
        + [pl.BlockSpec(memory_space=pl.ANY)] * len(chained),
        out_specs=pl.BlockSpec((owners, 1, rows, wide), lambda c: (0, offset + c, 0, 0)),
        out_shape=jax.ShapeDtypeStruct((owners, total, rows, wide), jnp.bfloat16),
        input_output_aliases={2: 0} if chained else {},
        compiler_params=params(),
        cost_estimate=scan_cost(count, owners * rows, heads),
        name="column_scan",
    )(pack, spare, *chained)


def row_kernel(rows, heads, counts, *refs):
    packs, spares = refs[: len(counts)], refs[len(counts) : -2]
    out_ref, held = refs[-2:]
    image, row = pl.program_id(0), pl.program_id(1)
    wide = heads * HEAD_DIM
    tall = held.shape[1] // PARTS
    length = held.shape[1] // rows
    units = [
        (pack, spare, k) for pack, spare, count in zip(packs, spares, counts) for k in range(count)
    ]

    for u, (pack, spare, k) in enumerate(units):

        @pl.when((row == 0) & (image == u // PARTS))
        def _(pack=pack, spare=spare, k=k, part=u % PARTS):
            depth = tall // pack.shape[0]
            lanes = pack.shape[2] // LANES
            here = slice(k * depth, (k + 1) * depth)
            for lane in range(lanes + 1):
                if lane < lanes:
                    block = pack[:, here, lane * LANES : (lane + 1) * LANES]
                else:
                    block = spare[:, here, :]
                held[lane, part * tall : (part + 1) * tall, :] = block.reshape(
                    tall, LANES
                ).astype(jnp.float32)

    def take(lane):
        return held[lane, pl.ds(row, length, stride=rows), :]

    def store(pair, result):
        out_ref[pair, pl.ds(row, length, stride=rows), :] = result

    first = wide // LANES
    scan_sequence(
        length,
        heads,
        *both_maps(take(first), take(first + 2)),
        take(first + 1).astype(jnp.bfloat16),
        take,
        store,
    )


def row_scan(packs, spares, counts, images, rows, columns, heads):
    packed = packs[0].shape[2]
    total = rows * columns
    wide = heads * HEAD_DIM
    return pl.pallas_call(
        functools.partial(row_kernel, rows, heads, counts),
        grid=(images, rows),
        in_specs=[resident(pack.shape, lambda i, r: (0, 0, 0)) for pack in packs + spares],
        out_specs=pl.BlockSpec((wide // LANES, total, LANES), lambda i, r: (0, i, 0)),
        out_shape=jax.ShapeDtypeStruct((wide // LANES, images * total, LANES), jnp.float32),
        scratch_shapes=[pltpu.VMEM((packed // LANES + 1, total, LANES), jnp.float32)],
        compiler_params=params(),
        cost_estimate=scan_cost(images * rows, columns, heads),
        name="row_scan",
    )(*packs, *spares)


def output_kernel(t_ref, row_ref, col_ref, inner_ref, skip_ref, gain_ref, w_own, w_other, own_ref, send_ref):
    tall, wide = inner_ref.shape
    group = NORM_HEADS * HEAD_DIM
    gated = []
    for start in range(0, wide, group):
        parts = []
        squares = 0.0
        for lane in range(start, start + group, LANES):
            part = slice(lane, lane + LANES)
            total = (
                row_ref[lane // LANES]
                + col_ref[:, :, part].astype(jnp.float32).reshape(tall, LANES)
                + skip_ref[:, part] * inner_ref[:, part].astype(jnp.float32)
            )
            parts.append(total)
            squares = squares + total * total
        scale = lax.rsqrt(jnp.sum(squares, axis=-1, keepdims=True) / group + EPS)
        for k, total in enumerate(parts):
            lane = start + k * LANES
            gated.append((total * scale * gain_ref[:, lane : lane + LANES]).astype(jnp.bfloat16))
    gated = jnp.concatenate(gated, axis=1)
    send_ref[...] = jnp.dot(gated, w_other[...], preferred_element_type=jnp.float32).astype(
        jnp.bfloat16
    )
    own_ref[...] = jnp.dot(gated, w_own[...], preferred_element_type=jnp.float32)


def output(row_out, start, count, col, inner, skip, gain, w_out, place):
    wide = inner.shape[1]
    feats = w_out.shape[1] // 2
    depth = col.shape[1] // count
    owners = col.shape[0]
    tile = owners * depth
    rows = tile * count
    row_spec = pl.BlockSpec((tile, wide), lambda i, t: (start + i, 0))
    out_spec = pl.BlockSpec((tile, feats), lambda i, t: (i, 0))
    return pl.pallas_call(
        output_kernel,
        grid_spec=pltpu.PrefetchScalarGridSpec(
            num_scalar_prefetch=1,
            grid=(count,),
            in_specs=[
                pl.BlockSpec((wide // LANES, tile, LANES), lambda i, t: (0, start + i, 0)),
                pl.BlockSpec((owners, depth, wide), lambda i, t: (0, i, 0)),
                row_spec,
                resident((1, wide), lambda i, t: (0, 0)),
                resident((1, wide), lambda i, t: (0, 0)),
                resident((wide, feats), lambda i, t: (0, t[0])),
                resident((wide, feats), lambda i, t: (0, 1 - t[0])),
            ],
            out_specs=[out_spec, out_spec],
        ),
        out_shape=[
            jax.ShapeDtypeStruct((rows, feats), jnp.float32),
            jax.ShapeDtypeStruct((rows, feats), jnp.bfloat16),
        ],
        compiler_params=params(),
        cost_estimate=pl.CostEstimate(
            flops=4 * rows * feats * wide, transcendentals=0, bytes_accessed=16 * 2**20
        ),
        name="output",
    )(place, row_out, col, inner, skip, gain, w_out, w_out)


def finish_kernel(rows, own_ref, got_ref, tok_ref, *rest):
    out_ref, held = rest[-2:]
    width = tok_ref.shape[2]
    for lane in range(tok_ref.shape[3] // LANES):
        part = slice(lane * LANES, (lane + 1) * LANES)
        held[lane] = own_ref[:, part] + got_ref[:, part].astype(jnp.float32)
        for row in range(rows):
            out_ref[0, row, :, part] = (
                tok_ref[0, row, :, part] + held[lane, pl.ds(row, width, stride=rows), :]
            ).astype(jnp.bfloat16)


def finish(own, got, tokens, start, count, earlier):
    _, rows, columns, feats = tokens.shape
    step = columns // PARTS
    flat = pl.BlockSpec((step * rows, feats), lambda k: (k, 0))
    chained = [] if earlier is None else [earlier]
    return pl.pallas_call(
        functools.partial(finish_kernel, rows),
        grid=(count,),
        in_specs=[flat, flat, grid_block(tokens, start)]
        + [pl.BlockSpec(memory_space=pl.ANY)] * len(chained),
        out_specs=grid_block(tokens, start),
        out_shape=jax.ShapeDtypeStruct(tokens.shape, jnp.bfloat16),
        scratch_shapes=[pltpu.VMEM((feats // LANES, step * rows, LANES), jnp.float32)],
        input_output_aliases={3: 0} if chained else {},
        compiler_params=params(),
        cost_estimate=pl.CostEstimate(
            flops=0, transcendentals=0, bytes_accessed=12 * count * step * rows * feats
        ),
        name="finish",
    )(own, got, tokens, *chained)


def pipelined(
    owners, tokens, in_gain, w_inner, w_bc, w_step, step_bias, decay_rate, skip, norm_gain, w_out
):
    images, rows, columns, _ = tokens.shape
    heads = w_step.shape[1]
    wide = w_inner.shape[1]
    swap = [(0, 1), (1, 0)]
    place = lax.axis_index("tensor").astype(jnp.int32).reshape(1)
    pad = LANES - heads
    w_small = jnp.concatenate([w_bc, jnp.pad(w_step, ((0, 0), (0, pad)))], axis=1)
    bias = jnp.pad(step_bias, (0, pad)).reshape(1, LANES)
    rate = jnp.pad(decay_rate, (0, pad)).reshape(1, LANES)
    skip_wide = jnp.repeat(skip, HEAD_DIM).reshape(1, wide)
    gain = norm_gain.reshape(1, wide)
    units = images * PARTS
    per_unit = columns // PARTS // owners
    there = groups_of((1, units // 2 - 1, units - units // 2))
    back = groups_of((units // 2, units // 4, units - units // 2 - units // 4))
    own, other, packs, spares, arrived, halves = [], [], [], [], [], []
    for start, count in there:
        own.append(turn(tokens, start, count))
    for g in range(len(there)):
        other.append(lax.ppermute(own[g], "tensor", swap))
    inner = None
    for g, (start, count) in enumerate(there):
        inner, pack, spare = project(
            own[g], other[g], in_gain, w_inner, w_small, bias, rate, place, heads, owners,
            start, count, units, inner,
        )
        packs.append(pack)
        spares.append(spare)
        block = lax.all_to_all(pack, "space", split_axis=0, concat_axis=0, tiled=True)
        arrived.append(block.reshape(owners, count * per_unit, rows, pack.shape[2]))
        half = lax.ppermute(block[:, :, wide : wide + STATE], "tensor", swap)
        halves.append(half.reshape(owners, count * per_unit, rows, STATE))
    counts = tuple(count for _, count in there)
    row_out = row_scan(packs, spares, counts, images, rows, columns, heads)
    columns_out = [None] * len(back)
    for g, (start, count) in enumerate(there):
        for k, (low, size) in enumerate(back):
            first, last = max(start, low), min(start + count, low + size)
            if first < last:
                columns_out[k] = column_scan(
                    arrived[g], halves[g], heads, (first - start) * per_unit, (last - first) * per_unit,
                    (first - low) * per_unit, size * per_unit, columns_out[k],
                )
    result = None
    for k, (start, count) in enumerate(back):
        block = columns_out[k].reshape(owners, count * per_unit * rows, wide)
        block = lax.all_to_all(block, "space", split_axis=0, concat_axis=0, tiled=True)
        kept, send = output(row_out, start, count, block, inner, skip_wide, gain, w_out, place)
        got = lax.ppermute(send, "tensor", swap)
        result = finish(kept, got, tokens, start, count, result)
    return result


def groups_of(counts):
    starts = [sum(counts[:k]) for k in range(len(counts))]
    return list(zip(starts, counts))


def fits(owners, tensor, tokens, heads):
    images, rows, columns, _ = tokens
    return (
        tensor == 2
        and images * PARTS == 8
        and rows == SUBLANES
        and columns % (PARTS * owners) == 0
        and owners * rows == columns == LANES
        and heads % NORM_HEADS == 0
        and heads % 2 == 0
        and heads <= LANES
        and STATE == LANES == 2 * HEAD_DIM
    )


def dispatch(owners, tensor, tokens, *rest):
    if fits(owners, tensor, tokens.shape, rest[3].shape[1]):
        return pipelined(owners, tokens, *rest)
    return on_device(tokens, *rest)


def solution(mesh):
    body = functools.partial(dispatch, mesh.shape["space"], mesh.shape["tensor"])
    return jax.shard_map(
        body,
        mesh=mesh,
        in_specs=(
            P(None, "space", None, "tensor"),
            P(),
            P(None, "tensor"),
            P(),
            P(None, "tensor"),
            P("tensor"),
            P("tensor"),
            P("tensor"),
            P("tensor"),
            P("tensor", None),
        ),
        out_specs=P(None, "space", None, "tensor"),
        check_vma=False,
    )
```
